256 devices in a mesh: expert: 32 (over y, z), mp: 8 (over x, core).
Axes of the slice: x: 4, y: 4, z: 8, core: 2. Of those that a mesh axis runs over, the one named last changes fastest.
Arguments:
- tokens: bfloat16 [4096, 3584], P('expert', 'mp'), may hold values from -6 to 6
- assignments: int32 [4096, 2], P('expert'), may hold values from 0 to 31, all different within a row; in each aligned block of 128 rows (0 to 127, 128 to 255, ...) at most 16 rows name the same one
- gate_probs: float32 [4096, 2], P('expert'), may hold values from 0.05 to 0.5
- expert_gate: bfloat16 [32, 3584, 2560], P('expert', None, 'mp'), may hold values from -0.09375 to 0.09375
- expert_up: bfloat16 [32, 3584, 2560], P('expert', None, 'mp'), may hold values from -0.09375 to 0.09375
- expert_down: bfloat16 [32, 2560, 3584], P('expert', 'mp'), may hold values from -0.125 to 0.125
- shared_gate: bfloat16 [3584, 10240], P('mp', 'expert'), may hold values from -0.09375 to 0.09375
- shared_up: bfloat16 [3584, 10240], P('mp', 'expert'), may hold values from -0.09375 to 0.09375
- shared_down_weight: bfloat16 [10240, 3584], P('expert', 'mp'), may hold values from -0.0625 to 0.0625
Outputs:
- layer_out: bfloat16 [4096, 3584], P('expert', 'mp')
The draws below stay inside these ranges and needn't reach their ends.
Inputs may be any that keep to these rules, and one draw needn't show every extreme that they name: `assignments`: each row names 2 different experts; among the 128 rows of one index of the expert axis (aligned blocks) no expert is named more than 16 times.
All inputs are finite; a program needn't handle non-finite values.
Results may differ from the reference program's by a relative error of at most 0.0075.
Values may be sent and summed in bfloat16 or wider, within the bound.
A program may use at most 128 MiB of HBM per device.

```python
import math
import jax
import jax.numpy as jnp
import numpy as np
from jax import lax

D = 3584
FF = 2560
FS = 10240
TOP = 2
TOK_DEV = 128
EXPERTS = 32
TOKENS = 4096
CAP = 16
N_EXPERT = 32
N_MP = 8


def block_scale(rng, shape, pieces, smallest, top_value):
    level = 1.0
    for dim, blocks in pieces:
        steps = jax.random.uniform(jax.random.fold_in(jax.random.fold_in(rng, 6), dim), (blocks,), jnp.float32, smallest / len(pieces), top_value / len(pieces))
        level = level * jnp.repeat(jnp.exp(steps), shape[dim] // blocks).reshape((-1,) + (1,) * (len(shape) - 1 - dim))
    return level


def shared_out(key, own, number, rows, amount, top, bound, skew):
    ranking = jax.random.permutation(key, amount)
    heavy_load, common = shares(amount, rows * top, bound, skew, True), shares(amount, rows * top, bound, skew, False)
    places = jnp.arange(amount)

    def named(sizes, turn):
        used = int((sizes > 0).sum())
        fixed = max(1, used // 4)
        shifted = fixed + (places - fixed + turn * (used - fixed)) % max(1, amount - fixed)
        return jnp.zeros((amount,), jnp.int32).at[ranking[jnp.where(places < fixed, places, shifted)]].set(jnp.asarray(sizes, jnp.int32))

    sizes = jnp.where(number % 4 == 0, named(heavy_load, number // 4), named(common, number - number // 4 - 1))
    mixed = jax.random.permutation(jax.random.fold_in(own, 3), amount)
    source_of, receiver = mixed[0:amount // 2 * 2:2], mixed[1:amount // 2 * 2:2]
    margin = jnp.minimum(sizes[source_of] - 1, bound - sizes[receiver]) // 2
    margin = jnp.where((source_of == ranking[0]) | (receiver == ranking[0]) | (sizes[receiver] == 0), 0, jnp.maximum(margin, 0))
    shifted = jax.random.randint(jax.random.fold_in(own, 4), (amount // 2,), 0, 1 << 20) % (margin + 1)
    sizes = sizes.at[source_of].add(-shifted).at[receiver].add(shifted)
    items = jnp.searchsorted(jnp.cumsum(sizes), jnp.arange(rows * top), side="right").astype(jnp.int32)
    grid = items.reshape(top, rows).T
    grid = grid[jax.random.permutation(jax.random.fold_in(own, 1), rows)]
    turn = jax.random.randint(jax.random.fold_in(own, 2), (rows, 1), 0, top)
    return jnp.take_along_axis(grid, (jnp.arange(top)[None, :] + turn) % top, axis=1)


def shares(count, total, bound, lean, full):
    loads = [(1 << 20) // math.isqrt(rank ** lean) + 1 for rank in range(1, count + 1)]
    largest = bound if full else min(bound, max(-(-total // count), total * loads[0] // sum(loads)))
    least = 1 if total - largest >= count - 1 else 0
    counts, surplus = [largest] + [least] * (count - 1), total - largest - least * (count - 1)
    while surplus > 0:
        candidates = [i for i in range(1, count) if counts[i] < largest] or [i for i in range(1, count) if counts[i] < bound]
        whole, left = sum([loads[i] for i in candidates]), surplus
        for i in candidates:
            addition = min(bound - counts[i], max(1, left * loads[i] // whole), surplus)
            counts[i] = counts[i] + addition
            surplus = surplus - addition
    return np.array(counts)


def gaussian(rng, shape, scale, most, pieces=(), held_as=jnp.bfloat16):
    level = block_scale(rng, shape, pieces, -0.22, 0.18) if pieces else 1.0
    result = jax.random.normal(rng, shape, jnp.float32) * scale * level
    return jnp.minimum(jnp.maximum(result, -most), most).astype(held_as)


def setup_inputs(seed: int = 0) -> dict:
    splits = jax.random.split(jax.random.key(seed), 10)
    tokens = gaussian(splits[0], (TOKENS, D), 1.0, 6.0, ((0, 32), (1, 8)))
    assignments_keys = jax.random.split(jax.random.fold_in(splits[1], 1), TOKENS // TOK_DEV)
    assignments_turns = jax.random.permutation(jax.random.fold_in(splits[1], 3), TOKENS // TOK_DEV)
    assignments = jax.vmap(lambda own, number: shared_out(jax.random.fold_in(splits[1], 2), own, number, TOK_DEV, EXPERTS, TOP, CAP, 2))(assignments_keys, assignments_turns).reshape((TOKENS, TOP))
    gate_probs = jnp.clip(0.05 + 0.45 * jax.random.uniform(splits[2], (TOKENS, TOP), jnp.float32) ** block_scale(splits[2], (TOKENS, TOP), ((0, 32),), -0.2, 0.2), 0.05, 0.5)
    expert_gate = gaussian(splits[3], (EXPERTS, D, FF), D ** -0.5, 0.09375, ((0, 32), (2, 8)))
    expert_up = gaussian(splits[4], (EXPERTS, D, FF), D ** -0.5, 0.09375, ((0, 32), (2, 8)))
    expert_down = gaussian(splits[5], (EXPERTS, FF, D), FF ** -0.5, 0.125, ((0, 32), (1, 8)))
    shared_gate = gaussian(splits[6], (D, FS), D ** -0.5, 0.09375, ((0, 8), (1, 32)))
    shared_up = gaussian(splits[7], (D, FS), D ** -0.5, 0.09375, ((0, 8), (1, 32)))
    shared_down_weight = gaussian(splits[8], (FS, D), FS ** -0.5, 0.0625, ((0, 32), (1, 8)))
    return {"tokens": tokens, "assignments": assignments, "gate_probs": gate_probs, "expert_gate": expert_gate, "expert_up": expert_up, "expert_down": expert_down, "shared_gate": shared_gate, "shared_up": shared_up, "shared_down_weight": shared_down_weight}


def slot_table(assignments):
    pair_ids = assignments.reshape(N_EXPERT, TOK_DEV * TOP)
    onehot = (pair_ids[:, :, None] == jnp.arange(EXPERTS, dtype=jnp.int32)[None, None, :]).astype(jnp.int32)
    rank_ids = jnp.cumsum(onehot, axis=1) - onehot
    return jnp.sum(rank_ids * onehot, axis=2).reshape(TOKENS, TOP).astype(jnp.int32)


def reference(tokens, assignments, gate_probs, expert_gate, expert_up, expert_down, shared_gate, shared_up, shared_down_weight):
    shared_gate_act = jnp.dot(tokens, shared_gate, preferred_element_type=jnp.float32)
    shared_up_act = jnp.dot(tokens, shared_up, preferred_element_type=jnp.float32)
    shared_hidden = (jax.nn.silu(shared_gate_act) * shared_up_act).astype(jnp.bfloat16)
    shared_result = jnp.dot(shared_hidden, shared_down_weight, preferred_element_type=jnp.float32)

    slot_ids = slot_table(assignments)
    blocks = (jnp.arange(TOKENS, dtype=jnp.int32) // TOK_DEV)[:, None]
    column = (blocks * CAP + slot_ids).astype(jnp.int32)
    token_ids = jnp.broadcast_to(jnp.arange(TOKENS, dtype=jnp.int32)[:, None], (TOKENS, TOP))
    source = jnp.zeros((EXPERTS, N_EXPERT * CAP), jnp.int32).at[assignments, column].set(token_ids)
    filled = jnp.zeros((EXPERTS, N_EXPERT * CAP), jnp.float32).at[assignments, column].set(1.0)
    group = FF // N_MP

    def expert_step(running, expert_id):
        gathered = tokens[source[expert_id]] * filled[expert_id][:, None].astype(jnp.bfloat16)
        gate_act = jnp.dot(gathered, expert_gate[expert_id], preferred_element_type=jnp.float32)
        up_act = jnp.dot(gathered, expert_up[expert_id], preferred_element_type=jnp.float32)
        hidden = (jax.nn.silu(gate_act) * up_act).astype(jnp.bfloat16)
        split_segments = hidden.reshape(N_EXPERT * CAP, N_MP, group).transpose(1, 0, 2).astype(jnp.float32)
        down_weight_pieces = expert_down[expert_id].reshape(N_MP, group, D).astype(jnp.float32)
        partial_sums_list = jnp.einsum("gnc,gcv->gnv", split_segments, down_weight_pieces, precision=lax.Precision.HIGHEST)
        rounded = lax.optimization_barrier(partial_sums_list.astype(jnp.bfloat16))
        output = jnp.sum(rounded.astype(jnp.float32), axis=0)
        chosen = (assignments == expert_id)
        weights = jnp.sum(jnp.where(chosen, gate_probs, jnp.zeros_like(gate_probs)), axis=1)
        position = jnp.sum(jnp.where(chosen, column, jnp.zeros_like(column)), axis=1).astype(jnp.int32)
        return running + weights[:, None] * output[position], None

    routed, _ = lax.scan(expert_step, jnp.zeros((TOKENS, D), jnp.float32), jnp.arange(EXPERTS, dtype=jnp.int32))
    return (shared_result + routed).astype(jnp.bfloat16)
```

```python
import functools
import heapq

import jax
import jax.numpy as jnp
from jax import lax
from jax.experimental import pallas as pl
from jax.experimental.pallas import tpu as pltpu
from jax.sharding import PartitionSpec as P

MESH = pl.DeviceIdType.MESH
BF = jnp.bfloat16
F32 = jnp.float32
NY, NZ, NX, NM = 4, 8, 4, 8
BLOCK = 128
PIECE = 16
FEAT = 3584
LOCAL = 448
WIDE = FEAT + 128
SLOTS = 64
SPLIT = 1536
RATE = 80e3
HOP = 1.8


def cut(lo, n):
    first = (n // 128) // 2 * 128
    return (lo, first), (lo + first, n - first)


def ring(index, offset, size):
    return lax.rem(index + (offset + size) % size, size)


class Place:
    def __init__(self):
        e = lax.axis_index("expert")
        self.m = lax.axis_index("mp")
        self.y, self.z = lax.div(e, NZ), lax.rem(e, NZ)
        self.x, self.c = lax.div(self.m, 2), lax.rem(self.m, 2)

    def at(self, axis, d):
        y, z, m = self.y, self.z, self.m
        if axis == "y":
            y = ring(y, d, NY)
        elif axis == "z":
            z = ring(z, d, NZ)
        elif axis == "x":
            m = ring(self.x, d, NX) * 2 + self.c
        else:
            m = self.x * 2 + 1 - self.c
        return (y * NZ + z, m)


def greet(peers, extra=()):
    barrier = pltpu.get_barrier_semaphore()
    for device in peers:
        pl.semaphore_signal(barrier, inc=1, device_id=device, device_id_type=MESH)
    for condition, device in extra:

        @pl.when(condition)
        def _():
            pl.semaphore_signal(barrier, inc=1, device_id=device, device_id_type=MESH)

    return barrier


class Wire:
    def __init__(self, place, send_sem, recv_sem):
        self.place, self.send_sem, self.recv_sem = place, send_sem, recv_sem
        self.count, self.queue, self.sent, self.free, self.now = 0, [], [], {}, 0.0

    def send(self, axis, d, src, dst, size, then):
        k = self.count
        self.count += 1
        copy = pltpu.make_async_remote_copy(
            src_ref=src,
            dst_ref=dst,
            send_sem=self.send_sem.at[k],
            recv_sem=self.recv_sem.at[k],
            device_id=self.place.at(axis, d),
            device_id_type=MESH,
        )
        copy.start()
        self.sent.append(copy)
        begin = max(self.now, self.free.get((axis, d), 0.0))
        end = begin + size * 2 / RATE
        self.free[(axis, d)] = end
        heapq.heappush(self.queue, (end + HOP, k, copy, then))

    def run(self):
        while self.queue:
            when, _, copy, then = heapq.heappop(self.queue)
            self.now = max(self.now, when)
            copy.wait_recv()
            if then is not None:
                then()

    def drain(self):
        for copy in self.sent:
            copy.wait_send()


def gather_kernel(
    tok_ref, wgu_ref, wd_ref, x_ref, gu_ref, down_ref, pieces, own, send_sem, recv_sem, part_send, part_recv, local_sem
):
    p = Place()
    y, z, m = p.y, p.z, p.m
    mine = z == m
    sources = [(y * NZ + m, q) for q in range(NM)]
    targets = [(y * NZ + r, z) for r in range(NZ)]
    neighbours = [p.at(a, d) for a, d in (("x", 1), ("x", -1), ("y", 1), ("y", -1), ("z", 1), ("z", -1), ("c", 1))]
    barrier = greet(
        neighbours, [(jnp.logical_not(jnp.logical_and(mine, m == q)), sources[q]) for q in range(NM)]
    )
    pl.semaphore_wait(barrier, len(neighbours) + NM - mine.astype(jnp.int32))

    for r in range(NZ):
        src = tok_ref.at[pl.ds(r * PIECE, PIECE), :]
        away = jnp.logical_not(jnp.logical_and(mine, z == r))

        @pl.when(away)
        def _():
            pltpu.make_async_remote_copy(
                src_ref=src,
                dst_ref=pieces.at[m],
                send_sem=part_send.at[r],
                recv_sem=part_recv.at[m],
                device_id=targets[r],
                device_id_type=MESH,
            ).start()

        @pl.when(jnp.logical_not(away))
        def _():
            pltpu.make_async_copy(src, pieces.at[m], part_recv.at[m]).start()

    keep_gu = pltpu.make_async_copy(wgu_ref, gu_ref.at[m], local_sem.at[0])
    keep_gu.start()
    keep_down = pltpu.make_async_copy(wd_ref, down_ref.at[m], local_sem.at[1])
    keep_down.start()

    wire = Wire(p, send_sem, recv_sem)

    def weights(own_ref, out, rows, width):
        size = rows * width * 2

        def block(xo, partner, lo, n):
            c = 1 - p.c if partner else p.c
            return out.at[ring(p.x, xo, NX) * 2 + c, pl.ds(lo, n), :]

        def share(xo, lo, n):
            wire.send("c", 1, block(xo, False, lo, n), block(xo, False, lo, n), size * n // rows, None)

        def arrived(d, xo, lo, n):
            def then():
                if abs(xo) == 1:
                    low, high = cut_rows(lo, n)
                    a, k = low if d == 1 else high
                    wire.send(
                        "x", d, block(xo, False, a, k), block(xo, False, a, k), size * k // rows, arrived(d, xo - d, a, k)
                    )
                share(xo, lo, n)

            return then

        for d in (1, -1):
            wire.send("x", d, own_ref, out.at[m], size, arrived(d, -d, 0, rows))
        wire.send("c", 1, own_ref, out.at[m], size, None)

    def cut_rows(lo, n):
        first = (n // 16) // 2 * 16
        return (lo, first), (lo + first, n - first)

    weights(wgu_ref, gu_ref, LOCAL, 640)
    weights(wd_ref, down_ref, 320, 512)

    for q in range(NM):
        pltpu.make_async_copy(pieces.at[q], pieces.at[q], part_recv.at[q]).wait()
    parts = [pieces[q][:, :LOCAL] for q in range(NM)]
    tail = jnp.concatenate([pieces[0][:, LOCAL:], jnp.zeros((PIECE, 64), BF)], axis=1)
    own[...] = jnp.concatenate(parts + [tail], axis=1)

    keep = pltpu.make_async_copy(own, x_ref.at[z, y], local_sem.at[2])
    keep.start()
    wire.now = 6.0

    def block(zo, yo, lo, n):
        return x_ref.at[ring(z, zo, NZ), ring(y, yo, NY), :, pl.ds(lo, n)]

    def forward(axis, d, zo, yo, lo, n, src=None):
        dst = block(zo, yo, lo, n)
        wire.send(axis, d, dst if src is None else src, dst, PIECE * n * 2, arrived(axis, d, zo, yo, lo, n))

    def arrived(axis, d, zo, yo, lo, n):
        if axis == "z":
            zo -= d
            dist, far = abs(zo), 4
        else:
            yo -= d
            dist, far = abs(yo), 2

        def then():
            if dist < far - 1:
                forward(axis, d, zo, yo, lo, n)
            elif dist == far - 1:
                low, high = cut(lo, n)
                forward(axis, d, zo, yo, *(low if d == 1 else high))
            if axis == "y" and lo < SPLIT:
                for s in (1, -1):
                    forward("z", s, zo, yo, lo, n)
            if axis == "z" and lo >= SPLIT:
                for s in (1, -1):
                    forward("y", s, zo, yo, lo, n)

        return then

    for axes, lo, n in ((("y", "z"), 0, SPLIT), (("z", "y"), SPLIT, WIDE - SPLIT)):
        for axis in axes:
            for d in (1, -1):
                forward(axis, d, 0, 0, lo, n, own.at[:, pl.ds(lo, n)])
    wire.run()
    keep_gu.wait()
    keep_down.wait()
    keep.wait()
    for r in range(NZ):

        @pl.when(jnp.logical_not(jnp.logical_and(mine, z == r)))
        def _():
            pltpu.make_async_copy(
                tok_ref.at[pl.ds(r * PIECE, PIECE), :], tok_ref.at[pl.ds(r * PIECE, PIECE), :], part_send.at[r]
            ).wait()

    wire.drain()


def spec(space):
    return pl.BlockSpec(memory_space=space)


VM = pltpu.VMEM
ANY = pl.ANY


def params(number):
    return pltpu.CompilerParams(collective_id=number, has_side_effects=True, vmem_limit_bytes=48 * 2**20)


def gather(tok, wgu, wd):
    return pl.pallas_call(
        gather_kernel,
        name="gather",
        out_shape=(
            jax.ShapeDtypeStruct((NZ, NY, PIECE, WIDE), BF),
            jax.ShapeDtypeStruct((NM, LOCAL, 640), BF),
            jax.ShapeDtypeStruct((NM, 320, LOCAL), BF),
        ),
        in_specs=[spec(VM)] * 3,
        out_specs=[spec(ANY)] * 3,
        scratch_shapes=[
            pltpu.VMEM((NM, PIECE, 512), BF),
            pltpu.VMEM((PIECE, WIDE), BF),
            pltpu.SemaphoreType.DMA((112,)),
            pltpu.SemaphoreType.DMA((112,)),
            pltpu.SemaphoreType.DMA((NZ,)),
            pltpu.SemaphoreType.DMA((NM,)),
            pltpu.SemaphoreType.DMA((3,)),
        ],
        compiler_params=params(0),
    )(tok, wgu, wd)


def slots_kernel(s_ref, out_ref, send_sem, recv_sem, local_sem):
    p = Place()
    neighbours = [p.at("x", 1), p.at("x", -1), p.at("c", 1)]
    barrier = greet(neighbours)
    pl.semaphore_wait(barrier, 3)
    wire = Wire(p, send_sem, recv_sem)
    keep = pltpu.make_async_copy(s_ref, out_ref.at[p.m], local_sem)
    keep.start()

    def block(xo, lo, n):
        return out_ref.at[ring(p.x, xo, NX) * 2 + p.c, :, pl.ds(lo, n)]

    def forward(axis, d, xo, lo, n, src=None):
        dst = block(xo, lo, n)
        then = arrived(d, xo - d, lo, n) if axis == "x" else None
        wire.send(axis, d, dst if src is None else src, dst, SLOTS * n * 2, then)

    def arrived(d, xo, lo, n):
        def then():
            if abs(xo) == 1:
                low, high = cut(lo, n)
                forward("x", d, xo, *(low if d == 1 else high))
            forward("c", 1, xo, lo, n)

        return then

    for d in (1, -1):
        for lo, n in cut(0, FEAT)[:: d]:
            forward("x", d, 0, lo, n, s_ref.at[:, pl.ds(lo, n)])
    forward("c", 1, 0, 0, FEAT, s_ref)
    wire.run()
    keep.wait()
    wire.drain()


def gather_slots(s):
    return pl.pallas_call(
        slots_kernel,
        name="gather_slots",
        out_shape=jax.ShapeDtypeStruct((NM, SLOTS, FEAT), BF),
        in_specs=[spec(VM)],
        out_specs=spec(VM),
        scratch_shapes=[
            pltpu.SemaphoreType.DMA((24,)),
            pltpu.SemaphoreType.DMA((24,)),
            pltpu.SemaphoreType.DMA,
        ],
        compiler_params=params(1),
    )(s)


def sum_slots_kernel(r_ref, out_ref, from_pair, from_x, held, send_sem, recv_sem):
    p = Place()
    neighbours = [p.at("x", 1), p.at("x", -1), p.at("c", 1)]
    barrier = greet(neighbours)
    pl.semaphore_wait(barrier, 3)
    wire = Wire(p, send_sem, recv_sem)
    low, high = cut(0, FEAT)

    def mine(xo):
        return r_ref[ring(p.x, xo, NX) * 2 + p.c].astype(F32)

    landed = {1: None, -1: None}

    def far():
        held[2] = (mine(2) + from_pair[2].astype(F32)).astype(BF)
        for d, (lo, n) in ((1, low), (-1, high)):
            at = pl.ds(lo, n)
            wire.send("x", d, held.at[2, :, at], from_x.at[0 if d == 1 else 1, :, at], SLOTS * n * 2, passed(d, lo, n))

    ready = {}

    def near(d):
        def then():
            ready[(d, "pair")] = True
            onward(d)

        return then

    def passed(d, lo, n):
        def then():
            ready[(d, "far")] = (lo, n)
            onward(d)

        return then

    def onward(d):
        if (d, "pair") not in ready or (d, "far") not in ready:
            return
        slot = 1 if d == 1 else 3
        lo, n = ready[(d, "far")]
        k = 0 if d == 1 else 1
        total = mine(d) + from_pair[slot].astype(F32)
        held[slot] = total.astype(BF)
        at = pl.ds(lo, n)
        held[slot, :, at] = (total[:, lo : lo + n] + from_x[k, :, at].astype(F32)).astype(BF)
        wire.send("x", d, held.at[slot], from_x.at[2 + k], SLOTS * FEAT * 2, None)

    after = {2: far, 1: near(1), 3: near(-1), 0: None}
    for xo in (2, 1, 3, 0):
        src = r_ref.at[ring(p.x, xo, NX) * 2 + 1 - p.c]
        wire.send("c", 1, src, from_pair.at[xo], SLOTS * FEAT, after[xo])
    wire.run()
    out_ref[...] = mine(0) + from_pair[0].astype(F32) + from_x[2].astype(F32) + from_x[3].astype(F32)
    wire.drain()


def sum_slots(r):
    return pl.pallas_call(
        sum_slots_kernel,
        name="sum_slots",
        out_shape=jax.ShapeDtypeStruct((SLOTS, FEAT), F32),
        in_specs=[spec(VM)],
        out_specs=spec(VM),
        scratch_shapes=[
            pltpu.VMEM((NX, SLOTS, FEAT), BF),
            pltpu.VMEM((4, SLOTS, FEAT), BF),
            pltpu.VMEM((4, SLOTS, FEAT), BF),
            pltpu.SemaphoreType.DMA((16,)),
            pltpu.SemaphoreType.DMA((16,)),
        ],
        compiler_params=params(2),
    )(r)


def reduce_kernel(
    in_ref, out_ref, held, z_in, y_in, pieces, send_sem, recv_sem, part_send, part_recv
):
    p = Place()
    y, z, m = p.y, p.z, p.m
    mine = z == m
    sources = [(y * NZ + r, z) for r in range(NZ)]
    targets = [(y * NZ + m, q) for q in range(NM)]
    neighbours = [p.at(a, d) for a, d in (("y", 1), ("y", -1), ("z", 1), ("z", -1))]
    barrier = greet(
        neighbours, [(jnp.logical_not(jnp.logical_and(mine, z == r)), sources[r]) for r in range(NZ)]
    )
    pl.semaphore_wait(barrier, len(neighbours) + NM - mine.astype(jnp.int32))
    wire = Wire(p, send_sem, recv_sem)

    def index(zo, yo):
        return ring(z, zo, NZ), ring(y, yo, NY)

    sizes = {"z": NZ, "y": NY}
    inbox = {"z": z_in, "y": y_in}

    class Chain:
        def __init__(self, axis, other, lo, n, second, done):
            self.axis, self.other, self.lo, self.n = axis, other, lo, n
            self.second, self.done, self.left = second, done, 2
            self.far = sizes[axis] // 2
            self.ready = {}

        def where(self, o):
            return (o, self.other) if self.axis == "z" else (self.other, o)

        def mailbox(self, d, left, lo, n):
            zo, yo = self.where(0)
            k = (0 if d == 1 else 1) * self.far + left
            other = self.other % (NY if self.axis == "z" else NZ)
            return inbox[self.axis].at[k, other, :, pl.ds(lo, n)]

        def source(self, o, lo, n):
            a, b = index(*self.where(o))
            ref = held if self.second else in_ref
            return ref.at[a, b, :, pl.ds(lo, n)]

        def have(self, o):
            self.ready[o % sizes[self.axis]] = True
            if o % sizes[self.axis] == self.far:
                low, high = cut(self.lo, self.n)
                for d, (lo, n) in ((1, low), (-1, high)):
                    wire.send(
                        self.axis,
                        d,
                        self.source(self.far, lo, n),
                        self.mailbox(d, self.far - 1, lo, n),
                        PIECE * n * 2,
                        self.arrived(d, self.far - 1, lo, n),
                    )
            for d in (1, -1):
                self.step(d, o * d % sizes[self.axis])

        def arrived(self, d, left, lo, n):
            def then():
                self.ready[(d, left)] = (lo, n)
                self.step(d, left)

            return then

        def step(self, d, left):
            size = sizes[self.axis]
            o = d * left
            if left == 0 or left >= self.far:
                if left == 0:
                    self.finish()
                return
            if (d, left) not in self.ready or o % size not in self.ready:
                return
            lo, n = self.ready[(d, left)]
            a, b = index(*self.where(o))
            at = pl.ds(lo, n)
            base = held if self.second else in_ref
            if (lo, n) != (self.lo, self.n) and not self.second:
                rest = [c for c in cut(self.lo, self.n) if c != (lo, n)][0]
                held[a, b, :, pl.ds(*rest)] = in_ref[a, b, :, pl.ds(*rest)]
            total = base[a, b, :, at].astype(F32) + self.mailbox(d, left, lo, n)[...].astype(F32)
            held[a, b, :, at] = total.astype(BF)
            wire.send(
                self.axis,
                d,
                held.at[a, b, :, pl.ds(self.lo, self.n)],
                self.mailbox(d, left - 1, self.lo, self.n),
                PIECE * self.n * 2,
                self.arrived(d, left - 1, self.lo, self.n),
            )

        def finish(self):
            if (1, 0) not in self.ready or (-1, 0) not in self.ready or 0 not in self.ready or self.left == 0:
                return
            self.left = 0
            a, b = index(*self.where(0))
            at = pl.ds(self.lo, self.n)
            base = held if self.second else in_ref
            total = base[a, b, :, at].astype(F32)
            for d in (1, -1):
                total = total + self.mailbox(d, 0, self.lo, self.n)[...].astype(F32)
            if not self.second:
                held[a, b, :, at] = total.astype(BF)
            self.done(total)

    last = {}

    def plan(first, second, lo, n):
        def store(total):
            last[lo] = total

        final = Chain(second, 0, lo, n, True, store)
        far = sizes[second] // 2
        offsets = sorted(range(sizes[second]), key=lambda o: (-min(o, sizes[second] - o), o))
        chains = []
        for o in offsets:
            signed = o if o <= far else o - sizes[second]
            chains.append(Chain(first, signed, lo, n, False, lambda total, s=signed: final.have(s)))
        return chains

    groups = [plan("z", "y", 0, SPLIT), plan("y", "z", SPLIT, FEAT - SPLIT)]
    for group in groups:
        for chain in group:
            far = chain.far
            order = [far] + [s * d for d in range(far - 1, 0, -1) for s in (1, -1)] + [0]
            for o in order:
                chain.have(o)
    wire.run()
    whole = jnp.concatenate([last[0], last[SPLIT]], axis=1).astype(BF)
    for q in range(NM):
        pieces[q] = whole[:, q * LOCAL : (q + 1) * LOCAL]
    rows = pl.ds(pl.multiple_of(z * PIECE, PIECE), PIECE)
    for q in range(NM):
        away = jnp.logical_not(jnp.logical_and(mine, m == q))

        @pl.when(away)
        def _():
            pltpu.make_async_remote_copy(
                src_ref=pieces.at[q],
                dst_ref=out_ref.at[rows, :],
                send_sem=part_send.at[q],
                recv_sem=part_recv.at[z],
                device_id=targets[q],
                device_id_type=MESH,
            ).start()

        @pl.when(jnp.logical_not(away))
        def _():
            pltpu.make_async_copy(pieces.at[q], out_ref.at[rows, :], part_recv.at[z]).start()

    for r in range(NZ):
        pltpu.make_async_copy(pieces.at[r], pieces.at[r], part_recv.at[r]).wait()
    for q in range(NM):

        @pl.when(jnp.logical_not(jnp.logical_and(mine, m == q)))
        def _():
            pltpu.make_async_copy(pieces.at[q], pieces.at[q], part_send.at[q]).wait()

    wire.drain()


def reduce_out(partial):
    return pl.pallas_call(
        reduce_kernel,
        name="reduce_out",
        out_shape=jax.ShapeDtypeStruct((BLOCK, LOCAL), BF),
        in_specs=[spec(VM)],
        out_specs=spec(VM),
        scratch_shapes=[
            pltpu.VMEM((NZ, NY, PIECE, FEAT), BF),
            pltpu.VMEM((2 * (NZ // 2), NY, PIECE, FEAT), BF),
            pltpu.VMEM((2 * (NY // 2), NZ, PIECE, FEAT), BF),
            pltpu.VMEM((NM, PIECE, LOCAL), BF),
            pltpu.SemaphoreType.DMA((96,)),
            pltpu.SemaphoreType.DMA((96,)),
            pltpu.SemaphoreType.DMA((NM,)),
            pltpu.SemaphoreType.DMA((NZ,)),
        ],
        compiler_params=params(3),
    )(partial)


def dot(a, b):
    return jnp.dot(a, b, preferred_element_type=F32)


def rounded(v):
    return lax.reduce_precision(v, 8, 7)


def thirds(v):
    high = rounded(v)
    middle = rounded(v - high)
    return high, middle, v - high - middle


def on_device(tokens, assignments, gate_probs, expert_gate, expert_up, expert_down, shared_gate, shared_up, shared_down):
    me = lax.axis_index("expert").astype(F32)
    split = [part for k in range(2) for part in thirds(gate_probs[:, k : k + 1])]
    meta = jnp.concatenate([assignments.astype(F32)] + split + [jnp.zeros((BLOCK, 56), F32)], axis=1)
    tok = jnp.concatenate([tokens, meta.astype(BF)], axis=1)
    x, gu, down = gather(tok, jnp.concatenate([shared_gate, shared_up], axis=1), shared_down)
    x = x.reshape(NZ * NY * PIECE, WIDE)
    info = x[:, FEAT : FEAT + 8].astype(F32)
    x = x[:, :FEAT]
    rows = x.shape[0]

    named = (info[:, 0:2] == me).astype(F32)
    hit = named[:, 0] + named[:, 1]
    weight = named[:, 0] * (info[:, 2] + info[:, 3] + info[:, 4]) + named[:, 1] * (info[:, 5] + info[:, 6] + info[:, 7])
    t = jnp.arange(rows, dtype=jnp.int32)
    group = (t // PIECE) % NY
    before = ((t[:, None] < t[None, :]) & (group[:, None] == group[None, :])).astype(BF)
    rank = dot(hit.astype(BF)[None, :], before)[0]
    slot = jnp.where(hit > 0, group * 16 + rank.astype(jnp.int32), -1)
    place = slot[None, :] == jnp.arange(SLOTS, dtype=jnp.int32)[:, None]
    picked = dot(place.astype(BF), x).astype(BF)

    routed_in = gather_slots(picked).reshape(NM * SLOTS, FEAT)
    shared_act = dot(x, gu.reshape(FEAT, 640))
    shared_hidden = (jax.nn.silu(shared_act[:, :320]) * shared_act[:, 320:]).astype(BF)
    shared_out = dot(shared_hidden, jnp.moveaxis(down, 0, 1).reshape(320, FEAT))

    gate = dot(routed_in, expert_gate[0])
    up = dot(routed_in, expert_up[0])
    hidden = (jax.nn.silu(gate) * up).astype(BF)
    routed = dot(hidden, expert_down[0]).astype(BF)
    total = sum_slots(routed.reshape(NM, SLOTS, FEAT))

    scale = jnp.sum(place.astype(F32) * weight[None, :], axis=1)
    value = total * scale[:, None]
    back = place.astype(BF).T
    partial = shared_out + dot(back, value.astype(BF))
    return reduce_out(partial.astype(BF).reshape(NZ, NY, PIECE, FEAT))


def solution(mesh):
    placed = (
        P("expert", "mp"),
        P("expert", None),
        P("expert", None),
        P("expert", None, "mp"),
        P("expert", None, "mp"),
        P("expert", "mp", None),
        P("mp", "expert"),
        P("mp", "expert"),
        P("expert", "mp"),
    )
    return jax.shard_map(on_device, mesh=mesh, in_specs=placed, out_specs=P("expert", "mp"), check_vma=False)
```

```python
import heapq

import jax
import jax.numpy as jnp
from jax import lax
from jax.experimental import pallas as pl
from jax.experimental.pallas import tpu as pltpu
from jax.sharding import PartitionSpec as P

MESH = pl.DeviceIdType.MESH
BF = jnp.bfloat16
F32 = jnp.float32
NY, NZ, NX, NM = 4, 8, 4, 8
BLOCK = 128
PIECE = 16
FEAT = 3584
LOCAL = 448
WIDE = FEAT + 128
SLOTS = 64
SPLIT = 1536
RATE = 92e3
HOP = 2.6
LATE = 4.0


def cut(lo, n):
    first = (n // 128) // 2 * 128
    return (lo, first), (lo + first, n - first)


def ring(index, offset, size):
    return lax.rem(index + (offset + size) % size, size)


class Place:
    def __init__(self):
        e = lax.axis_index("expert")
        self.m = lax.axis_index("mp")
        self.y, self.z = lax.div(e, NZ), lax.rem(e, NZ)
        self.x, self.c = lax.div(self.m, 2), lax.rem(self.m, 2)

    def at(self, axis, d):
        y, z, m = self.y, self.z, self.m
        if axis == "y":
            y = ring(y, d, NY)
        elif axis == "z":
            z = ring(z, d, NZ)
        elif axis == "x":
            m = ring(self.x, d, NX) * 2 + self.c
        else:
            m = self.x * 2 + 1 - self.c
        return (y * NZ + z, m)


def greet(peers, extra=()):
    barrier = pltpu.get_barrier_semaphore()
    for device in peers:
        pl.semaphore_signal(barrier, inc=1, device_id=device, device_id_type=MESH)
    for condition, device in extra:

        @pl.when(condition)
        def _():
            pl.semaphore_signal(barrier, inc=1, device_id=device, device_id_type=MESH)

    return barrier


class Wire:
    def __init__(self, place, send_sem, recv_sem):
        self.place, self.send_sem, self.recv_sem = place, send_sem, recv_sem
        self.count, self.queue, self.sent, self.free, self.now = 0, [], [], {}, 0.0
        self.count_other = 0

    def send(self, axis, d, src, dst, size, then, late=0.0):
        k = self.count
        self.count += 1
        copy = pltpu.make_async_remote_copy(
            src_ref=src,
            dst_ref=dst,
            send_sem=self.send_sem.at[k],
            recv_sem=self.recv_sem.at[k],
            device_id=self.place.at(axis, d),
            device_id_type=MESH,
        )
        copy.start()
        self.sent.append(copy)
        begin = max(self.now, self.free.get((axis, d), 0.0))
        end = begin + size * 2 / RATE
        self.free[(axis, d)] = end
        heapq.heappush(self.queue, (end + HOP + late, k, copy, then))

    def push(self, when, then):
        self.count_other -= 1
        heapq.heappush(self.queue, (when, self.count_other, None, then))

    def run(self):
        while self.queue:
            when, _, copy, then = heapq.heappop(self.queue)
            self.now = max(self.now, when)
            if copy is not None:
                copy.wait_recv()
            if then is not None:
                then()

    def drain(self):
        for copy in self.sent:
            copy.wait_send()


def gather_kernel(
    tok_ref, wgu_ref, wd_ref, x_ref, gu_ref, down_ref, pieces, own, send_sem, recv_sem, part_send, part_recv, local_sem
):
    p = Place()
    y, z, m = p.y, p.z, p.m
    mine = z == m
    sources = [(y * NZ + m, q) for q in range(NM)]
    targets = [(y * NZ + r, z) for r in range(NZ)]
    neighbours = [p.at(a, d) for a, d in (("x", 1), ("x", -1), ("y", 1), ("y", -1), ("z", 1), ("z", -1), ("c", 1))]
    barrier = greet(
        neighbours, [(jnp.logical_not(jnp.logical_and(mine, m == q)), sources[q]) for q in range(NM)]
    )
    pl.semaphore_wait(barrier, len(neighbours) + NM - mine.astype(jnp.int32))

    for r in range(NZ):
        src = tok_ref.at[pl.ds(r * PIECE, PIECE), :]
        away = jnp.logical_not(jnp.logical_and(mine, z == r))

        @pl.when(away)
        def _():
            pltpu.make_async_remote_copy(
                src_ref=src,
                dst_ref=pieces.at[m],
                send_sem=part_send.at[r],
                recv_sem=part_recv.at[m],
                device_id=targets[r],
                device_id_type=MESH,
            ).start()

        @pl.when(jnp.logical_not(away))
        def _():
            pltpu.make_async_copy(src, pieces.at[m], part_recv.at[m]).start()

    keep_gu = pltpu.make_async_copy(wgu_ref, gu_ref.at[m], local_sem.at[0])
    keep_gu.start()
    keep_down = pltpu.make_async_copy(wd_ref, down_ref.at[m], local_sem.at[1])
    keep_down.start()

    wire = Wire(p, send_sem, recv_sem)

    def weights(own_ref, out, rows, width):
        size = rows * width * 2

        def block(xo, lo, n):
            return out.at[ring(p.x, xo, NX) * 2 + p.c, pl.ds(lo, n), :]

        half = cut_rows(0, rows)

        def share(xo, lo, n):
            at = block(xo, lo, n)
            wire.send("c", 1, at, at, size * n // rows // 4, None, 2 * LATE)

        def arrived(d, xo, lo, n):
            def then():
                if abs(xo) == 1 and (lo, n) == half[0 if d == 1 else 1]:
                    at = block(xo, lo, n)
                    wire.send("x", d, at, at, size * n // rows, arrived(d, xo - d, lo, n), LATE)
                share(xo, lo, n)

            return then

        def begin(first):
            for d in (1, -1):
                lo, n = half[0 if (d == 1) == first else 1]
                src = own_ref.at[pl.ds(lo, n), :]
                wire.send("x", d, src, block(0, lo, n), size * n // rows, arrived(d, -d, lo, n), LATE)
            if first:
                wire.send("c", 1, own_ref, out.at[m], size // 4, None, 2 * LATE)

        return begin

    def cut_rows(lo, n):
        first = (n // 16) // 2 * 16
        return (lo, first), (lo + first, n - first)

    sends = [weights(wgu_ref, gu_ref, LOCAL, 640), weights(wd_ref, down_ref, 320, 512)]

    for q in range(NM):
        pltpu.make_async_copy(pieces.at[q], pieces.at[q], part_recv.at[q]).wait()
    parts = [pieces[q][:, :LOCAL] for q in range(NM)]
    tail = jnp.concatenate([pieces[0][:, LOCAL:], jnp.zeros((PIECE, 64), BF)], axis=1)
    own[...] = jnp.concatenate(parts + [tail], axis=1)

    keep = pltpu.make_async_copy(own, x_ref.at[z, y], local_sem.at[2])
    keep.start()
    wire.now = 6.0
    for first in (True, False):
        for begin in sends:
            begin(first)

    def block(zo, yo, lo, n):
        return x_ref.at[ring(z, zo, NZ), ring(y, yo, NY), :, pl.ds(lo, n)]

    def forward(axis, d, zo, yo, lo, n, src=None):
        dst = block(zo, yo, lo, n)
        wire.send(axis, d, dst if src is None else src, dst, PIECE * n * 2, arrived(axis, d, zo, yo, lo, n))

    def arrived(axis, d, zo, yo, lo, n):
        if axis == "z":
            zo -= d
            dist, far = abs(zo), 4
        else:
            yo -= d
            dist, far = abs(yo), 2

        def then():
            if dist < far - 1:
                forward(axis, d, zo, yo, lo, n)
            elif dist == far - 1:
                low, high = cut(lo, n)
                forward(axis, d, zo, yo, *(low if d == 1 else high))
            if axis == "y" and lo < SPLIT:
                for s in (1, -1):
                    forward("z", s, zo, yo, lo, n)
            if axis == "z" and lo >= SPLIT:
                for s in (1, -1):
                    forward("y", s, zo, yo, lo, n)

        return then

    for axes, lo, n in ((("y", "z"), 0, SPLIT), (("z", "y"), SPLIT, WIDE - SPLIT)):
        for axis in axes:
            for d in (1, -1):
                forward(axis, d, 0, 0, lo, n, own.at[:, pl.ds(lo, n)])
    wire.run()
    keep_gu.wait()
    keep_down.wait()
    keep.wait()
    for r in range(NZ):

        @pl.when(jnp.logical_not(jnp.logical_and(mine, z == r)))
        def _():
            pltpu.make_async_copy(
                tok_ref.at[pl.ds(r * PIECE, PIECE), :], tok_ref.at[pl.ds(r * PIECE, PIECE), :], part_send.at[r]
            ).wait()

    wire.drain()


def spec(space):
    return pl.BlockSpec(memory_space=space)


VM = pltpu.VMEM
ANY = pl.ANY


def params(number):
    return pltpu.CompilerParams(collective_id=number, has_side_effects=True, vmem_limit_bytes=48 * 2**20)


def gather(tok, wgu, wd):
    return pl.pallas_call(
        gather_kernel,
        name="gather",
        out_shape=(
            jax.ShapeDtypeStruct((NZ, NY, PIECE, WIDE), BF),
            jax.ShapeDtypeStruct((NM, LOCAL, 640), BF),
            jax.ShapeDtypeStruct((NM, 320, LOCAL), BF),
        ),
        in_specs=[spec(VM)] * 3,
        out_specs=[spec(ANY)] * 3,
        scratch_shapes=[
            pltpu.VMEM((NM, PIECE, 512), BF),
            pltpu.VMEM((PIECE, WIDE), BF),
            pltpu.SemaphoreType.DMA((128,)),
            pltpu.SemaphoreType.DMA((128,)),
            pltpu.SemaphoreType.DMA((NZ,)),
            pltpu.SemaphoreType.DMA((NM,)),
            pltpu.SemaphoreType.DMA((3,)),
        ],
        compiler_params=params(0),
    )(tok, wgu, wd)


ROWS = 2 * SLOTS
OFFSETS = (0, 1, 3, 2)


def experts_kernel(
    s_ref, back_ref, scale_ref, x_hbm, gu_hbm, wd_hbm, eg_hbm, eu_hbm, ed_hbm, out_ref,
    shared, value, rows, eg, eu, ed, xs, gu, wd, wide, part, from_pair, from_x, held, send_sem, recv_sem, local_sem, load_sem,
):
    p = Place()
    loads = [
        pltpu.make_async_copy(src, dst, load_sem.at[k])
        for k, (src, dst) in enumerate(
            ((eg_hbm, eg), (eu_hbm, eu), (ed_hbm, ed), (wd_hbm, wd), (gu_hbm, gu), (x_hbm, xs))
        )
    ]
    for load in loads:
        load.start()
    neighbours = [p.at("x", 1), p.at("x", -1), p.at("c", 1)]
    barrier = greet(neighbours)
    pl.semaphore_wait(barrier, 3)
    wire = Wire(p, send_sem, recv_sem)
    wire.now = 3.0
    keep = pltpu.make_async_copy(s_ref, rows.at[p.m], local_sem)
    keep.start()
    low, high = cut(0, FEAT)

    def block(xo, lo, n):
        return rows.at[ring(p.x, xo, NX) * 2 + p.c, :, pl.ds(lo, n)]

    def base(xo):
        return ring(p.x, xo, NX) * 2

    missing = {0: 1, 1: 4, 3: 4, 2: 4}

    def landed(xo):
        def then():
            missing[xo] -= 1
            if missing[xo] == 0:
                routed(xo)

        return then

    def share(xo, lo, n):
        wire.send("c", 1, block(xo, lo, n), block(xo, lo, n), SLOTS * n, landed(xo % NX))

    def moved(d, xo, lo, n):
        def then():
            if abs(xo) == 1 and (lo, n) == (low if d == 1 else high):
                dst = block(xo, lo, n)
                wire.send("x", d, dst, dst, SLOTS * n * 2, moved(d, xo - d, lo, n))
                if d == -1:
                    wire.push(wire.now, lambda: filler(1, 1))
            share(xo, lo, n)
            landed(xo % NX)()

        return then

    for first in (True, False):
        for d in (1, -1):
            lo, n = low if (d == 1) == first else high
            wire.send("x", d, s_ref.at[:, pl.ds(lo, n)], block(0, lo, n), SLOTS * n * 2, moved(d, -d, lo, n))
        if first:
            wire.send("c", 1, s_ref, rows.at[p.m], SLOTS * FEAT // 2, landed(0))

    def turned(a, b):
        return lax.dot_general(a, b, (((1,), (1,)), ((), ())), preferred_element_type=F32)

    def routed(xo):
        if xo == 0:
            keep.wait()
            for load in loads[:3]:
                load.wait()
        chunk = rows[pl.ds(base(xo), 2)].reshape(ROWS, FEAT)
        hidden = (jax.nn.silu(turned(chunk, eg[...])) * turned(chunk, eu[...])).astype(BF)
        part[xo] = dot(hidden, ed[...]).astype(BF).reshape(2, SLOTS, FEAT)
        wire.now += 2.5
        wire.send("c", 1, part.at[xo, 1 - p.c], from_pair.at[xo], SLOTS * FEAT // 2, paired(xo))
        if xo == 0:
            filler(0, 1)
        if xo == 2:
            wire.push(wire.now + 5.0, lambda: filler(2, 2))

    def filler(start, count):
        if start == 0:
            for load in loads[3:]:
                load.wait()
            wide[...] = jnp.concatenate([wd[q] for q in range(NM)], axis=1)

        def body(i, carry):
            at = pl.ds(pl.multiple_of(i * ROWS, ROWS), ROWS)
            both = dot(xs[at, :FEAT], gu[...])
            hidden = (jax.nn.silu(both[:, :320]) * both[:, 320:640]).astype(BF)
            shared[at, :] = dot(hidden, wide[...])
            return carry

        lax.fori_loop(start, start + count, body, 0)
        wire.now += 2.5 * count

    def own_sum(xo):
        return part[xo, p.c].astype(F32) + from_pair[xo].astype(F32)

    ready = {}

    def paired(xo):
        def then():
            if xo == 0:
                return
            held[xo] = own_sum(xo).astype(BF)
            for d in (1, -1):
                lo, n = low if d == 1 else high
                k = 0 if d == 1 else 1
                if xo == 2:
                    at = pl.ds(lo, n)
                    wire.send("x", d, held.at[2, :, at], from_x.at[k, :, at], SLOTS * n * 2, passed(d, lo, n))
                elif xo == d % NX:
                    lo, n = high if d == 1 else low
                    at = pl.ds(lo, n)
                    wire.send("x", d, held.at[xo, :, at], from_x.at[2 + k, :, at], SLOTS * n * 2, None)
                    ready[(d, "pair")] = True
                    onward(d)

        return then

    def passed(d, lo, n):
        def then():
            ready[(d, "far")] = (lo, n)
            onward(d)

        return then

    def onward(d):
        if (d, "pair") not in ready or (d, "far") not in ready:
            return
        slot = d % NX
        lo, n = ready[(d, "far")]
        k = 0 if d == 1 else 1
        at = pl.ds(lo, n)
        total = part[slot, p.c, :, at].astype(F32) + from_pair[slot, :, at].astype(F32) + from_x[k, :, at].astype(F32)
        held[slot, :, at] = total.astype(BF)
        wire.send("x", d, held.at[slot, :, at], from_x.at[2 + k, :, at], SLOTS * n * 2, None)

    wire.run()
    total = own_sum(0) + from_x[2].astype(F32) + from_x[3].astype(F32)
    value[...] = (total * scale_ref[...]).astype(BF)

    def combine(i, carry):
        at = pl.ds(pl.multiple_of(i * ROWS, ROWS), ROWS)
        out_ref[at, :] = (shared[at, :] + dot(back_ref[at, :], value[...])).astype(BF)
        return carry

    lax.fori_loop(0, 4, combine, 0)
    wire.drain()


def experts(s, back, scale, x, gu, wd, eg, eu, ed):
    slots = pltpu.VMEM((NX, SLOTS, FEAT), BF)
    return pl.pallas_call(
        experts_kernel,
        name="experts",
        out_shape=jax.ShapeDtypeStruct((4 * BLOCK, FEAT), BF),
        in_specs=[spec(VM)] * 3 + [spec(ANY)] * 6,
        out_specs=spec(VM),
        scratch_shapes=[
            pltpu.VMEM((4 * BLOCK, FEAT), F32),
            pltpu.VMEM((SLOTS, FEAT), BF),
            pltpu.VMEM((NM, SLOTS, FEAT), BF),
            pltpu.VMEM((320, FEAT), BF),
            pltpu.VMEM((320, FEAT), BF),
            pltpu.VMEM((320, FEAT), BF),
            pltpu.VMEM((4 * BLOCK, WIDE), BF),
            pltpu.VMEM((FEAT, 640), BF),
            pltpu.VMEM((NM, 320, LOCAL), BF),
            pltpu.VMEM((320, FEAT), BF),
            pltpu.VMEM((NX, 2, SLOTS, FEAT), BF),
            slots,
            slots,
            slots,
            pltpu.SemaphoreType.DMA((32,)),
            pltpu.SemaphoreType.DMA((32,)),
            pltpu.SemaphoreType.DMA,
            pltpu.SemaphoreType.DMA((6,)),
        ],
        compiler_params=params(1),
    )(s, back, scale, x, gu, wd, eg, eu, ed)


def reduce_kernel(
    in_ref, out_ref, held, z_in, y_in, pieces, send_sem, recv_sem, part_send, part_recv
):
    p = Place()
    y, z, m = p.y, p.z, p.m
    mine = z == m
    sources = [(y * NZ + r, z) for r in range(NZ)]
    targets = [(y * NZ + m, q) for q in range(NM)]
    neighbours = [p.at(a, d) for a, d in (("y", 1), ("y", -1), ("z", 1), ("z", -1))]
    barrier = greet(
        neighbours, [(jnp.logical_not(jnp.logical_and(mine, z == r)), sources[r]) for r in range(NZ)]
    )
    pl.semaphore_wait(barrier, len(neighbours) + NM - mine.astype(jnp.int32))
    wire = Wire(p, send_sem, recv_sem)

    def index(zo, yo):
        return ring(z, zo, NZ), ring(y, yo, NY)

    sizes = {"z": NZ, "y": NY}
    inbox = {"z": z_in, "y": y_in}

    class Chain:
        def __init__(self, axis, other, lo, n, second, done):
            self.axis, self.other, self.lo, self.n = axis, other, lo, n
            self.second, self.done, self.left = second, done, 2
            self.far = sizes[axis] // 2
            self.ready = {}

        def where(self, o):
            return (o, self.other) if self.axis == "z" else (self.other, o)

        def mailbox(self, d, left, lo, n):
            zo, yo = self.where(0)
            k = (0 if d == 1 else 1) * self.far + left
            other = self.other % (NY if self.axis == "z" else NZ)
            return inbox[self.axis].at[k, other, :, pl.ds(lo, n)]

        def source(self, o, lo, n):
            a, b = index(*self.where(o))
            ref = held if self.second else in_ref
            return ref.at[a, b, :, pl.ds(lo, n)]

        def have(self, o):
            self.ready[o % sizes[self.axis]] = True
            if o % sizes[self.axis] == self.far:
                low, high = cut(self.lo, self.n)
                for d, (lo, n) in ((1, low), (-1, high)):
                    wire.send(
                        self.axis,
                        d,
                        self.source(self.far, lo, n),
                        self.mailbox(d, self.far - 1, lo, n),
                        PIECE * n * 2,
                        self.arrived(d, self.far - 1, lo, n),
                    )
            for d in (1, -1):
                self.step(d, o * d % sizes[self.axis])

        def arrived(self, d, left, lo, n):
            def then():
                self.ready[(d, left)] = (lo, n)
                self.step(d, left)

            return then

        def step(self, d, left):
            size = sizes[self.axis]
            o = d * left
            if left == 0 or left >= self.far:
                if left == 0:
                    self.finish()
                return
            if (d, left) not in self.ready or o % size not in self.ready:
                return
            lo, n = self.ready[(d, left)]
            a, b = index(*self.where(o))
            at = pl.ds(lo, n)
            base = held if self.second else in_ref
            if (lo, n) != (self.lo, self.n) and not self.second:
                rest = [c for c in cut(self.lo, self.n) if c != (lo, n)][0]
                held[a, b, :, pl.ds(*rest)] = in_ref[a, b, :, pl.ds(*rest)]
            total = base[a, b, :, at].astype(F32) + self.mailbox(d, left, lo, n)[...].astype(F32)
            held[a, b, :, at] = total.astype(BF)
            wire.send(
                self.axis,
                d,
                held.at[a, b, :, pl.ds(self.lo, self.n)],
                self.mailbox(d, left - 1, self.lo, self.n),
                PIECE * self.n * 2,
                self.arrived(d, left - 1, self.lo, self.n),
            )

        def finish(self):
            if (1, 0) not in self.ready or (-1, 0) not in self.ready or 0 not in self.ready or self.left == 0:
                return
            self.left = 0
            a, b = index(*self.where(0))
            at = pl.ds(self.lo, self.n)
            base = held if self.second else in_ref
            total = base[a, b, :, at].astype(F32)
            for d in (1, -1):
                total = total + self.mailbox(d, 0, self.lo, self.n)[...].astype(F32)
            if not self.second:
                held[a, b, :, at] = total.astype(BF)
            self.done(total)

    last = {}

    def plan(first, second, lo, n):
        def store(total):
            last[lo] = total

        final = Chain(second, 0, lo, n, True, store)
        far = sizes[second] // 2
        offsets = sorted(range(sizes[second]), key=lambda o: (-min(o, sizes[second] - o), o))
        chains = []
        for o in offsets:
            signed = o if o <= far else o - sizes[second]
            chains.append(Chain(first, signed, lo, n, False, lambda total, s=signed: final.have(s)))
        return chains

    groups = [plan("z", "y", 0, SPLIT), plan("y", "z", SPLIT, FEAT - SPLIT)]
    for group in groups:
        for chain in group:
            far = chain.far
            order = [far] + [s * d for d in range(far - 1, 0, -1) for s in (1, -1)] + [0]
            for o in order:
                chain.have(o)
    wire.run()
    whole = jnp.concatenate([last[0], last[SPLIT]], axis=1).astype(BF)
    for q in range(NM):
        pieces[q] = whole[:, q * LOCAL : (q + 1) * LOCAL]
    rows = pl.ds(pl.multiple_of(z * PIECE, PIECE), PIECE)
    for q in range(NM):
        away = jnp.logical_not(jnp.logical_and(mine, m == q))

        @pl.when(away)
        def _():
            pltpu.make_async_remote_copy(
                src_ref=pieces.at[q],
                dst_ref=out_ref.at[rows, :],
                send_sem=part_send.at[q],
                recv_sem=part_recv.at[z],
                device_id=targets[q],
                device_id_type=MESH,
            ).start()

        @pl.when(jnp.logical_not(away))
        def _():
            pltpu.make_async_copy(pieces.at[q], out_ref.at[rows, :], part_recv.at[z]).start()

    for r in range(NZ):
        pltpu.make_async_copy(pieces.at[r], pieces.at[r], part_recv.at[r]).wait()
    for q in range(NM):

        @pl.when(jnp.logical_not(jnp.logical_and(mine, m == q)))
        def _():
            pltpu.make_async_copy(pieces.at[q], pieces.at[q], part_send.at[q]).wait()

    wire.drain()


def reduce_out(partial):
    return pl.pallas_call(
        reduce_kernel,
        name="reduce_out",
        out_shape=jax.ShapeDtypeStruct((BLOCK, LOCAL), BF),
        in_specs=[spec(VM)],
        out_specs=spec(VM),
        scratch_shapes=[
            pltpu.VMEM((NZ, NY, PIECE, FEAT), BF),
            pltpu.VMEM((2 * (NZ // 2), NY, PIECE, FEAT), BF),
            pltpu.VMEM((2 * (NY // 2), NZ, PIECE, FEAT), BF),
            pltpu.VMEM((NM, PIECE, LOCAL), BF),
            pltpu.SemaphoreType.DMA((96,)),
            pltpu.SemaphoreType.DMA((96,)),
            pltpu.SemaphoreType.DMA((NM,)),
            pltpu.SemaphoreType.DMA((NZ,)),
        ],
        compiler_params=params(3),
    )(partial)


def dot(a, b):
    return jnp.dot(a, b, preferred_element_type=F32)


def rounded(v):
    return lax.reduce_precision(v, 8, 7)


def thirds(v):
    high = rounded(v)
    middle = rounded(v - high)
    return high, middle, v - high - middle


def on_device(tokens, assignments, gate_probs, expert_gate, expert_up, expert_down, shared_gate, shared_up, shared_down):
    me = lax.axis_index("expert").astype(F32)
    split = [part for k in range(2) for part in thirds(gate_probs[:, k : k + 1])]
    meta = jnp.concatenate([assignments.astype(F32)] + split + [jnp.zeros((BLOCK, 56), F32)], axis=1)
    tok = jnp.concatenate([tokens, meta.astype(BF)], axis=1)
    x, gu, down = gather(tok, jnp.concatenate([shared_gate, shared_up], axis=1), shared_down)
    wide_x = x.reshape(NZ * NY * PIECE, WIDE)
    info = wide_x[:, FEAT : FEAT + 8].astype(F32)
    x = wide_x[:, :FEAT]
    rows = x.shape[0]

    named = (info[:, 0:2] == me).astype(F32)
    hit = named[:, 0] + named[:, 1]
    weight = named[:, 0] * (info[:, 2] + info[:, 3] + info[:, 4]) + named[:, 1] * (info[:, 5] + info[:, 6] + info[:, 7])
    t = jnp.arange(rows, dtype=jnp.int32)
    group = (t // PIECE) % NY
    before = ((t[:, None] < t[None, :]) & (group[:, None] == group[None, :])).astype(BF)
    rank = dot(hit.astype(BF)[None, :], before)[0]
    slot = jnp.where(hit > 0, group * 16 + rank.astype(jnp.int32), -1)
    place = slot[None, :] == jnp.arange(SLOTS, dtype=jnp.int32)[:, None]
    picked = dot(place.astype(BF), x).astype(BF)

    scale = jnp.sum(place.astype(F32) * weight[None, :], axis=1)
    back = slot[:, None] == jnp.arange(SLOTS, dtype=jnp.int32)[None, :]
    partial = experts(
        picked,
        back.astype(BF),
        scale[:, None],
        wide_x,
        gu.reshape(FEAT, 640),
        down,
        jnp.swapaxes(expert_gate[0], 0, 1),
        jnp.swapaxes(expert_up[0], 0, 1),
        expert_down[0],
    )
    return reduce_out(partial.reshape(NZ, NY, PIECE, FEAT))


def solution(mesh):
    placed = (
        P("expert", "mp"),
        P("expert", None),
        P("expert", None),
        P("expert", None, "mp"),
        P("expert", None, "mp"),
        P("expert", "mp", None),
        P("mp", "expert"),
        P("mp", "expert"),
        P("expert", "mp"),
    )
    return jax.shard_map(on_device, mesh=mesh, in_specs=placed, out_specs=P("expert", "mp"), check_vma=False)
```

```python
import heapq

import jax
import jax.numpy as jnp
from jax import lax
from jax.experimental import pallas as pl
from jax.experimental.pallas import tpu as pltpu
from jax.sharding import PartitionSpec as P

MESH = pl.DeviceIdType.MESH
BF = jnp.bfloat16
F32 = jnp.float32
NY, NZ, NX, NM = 4, 8, 4, 8
BLOCK = 128
PIECE = 16
FEAT = 3584
LOCAL = 448
WIDE = FEAT + 128
SLOTS = 64
SPLIT = 1536
RATE = 92e3
HOP = 2.6
LATE = 4.0


def cut(lo, n):
    first = (n // 128) // 2 * 128
    return (lo, first), (lo + first, n - first)


def ring(index, offset, size):
    return lax.rem(index + (offset + size) % size, size)


class Place:
    def __init__(self):
        e = lax.axis_index("expert")
        self.m = lax.axis_index("mp")
        self.y, self.z = lax.div(e, NZ), lax.rem(e, NZ)
        self.x, self.c = lax.div(self.m, 2), lax.rem(self.m, 2)

    def at(self, axis, d):
        y, z, m = self.y, self.z, self.m
        if axis == "y":
            y = ring(y, d, NY)
        elif axis == "z":
            z = ring(z, d, NZ)
        elif axis == "x":
            m = ring(self.x, d, NX) * 2 + self.c
        else:
            m = self.x * 2 + 1 - self.c
        return (y * NZ + z, m)


def greet(peers, extra=()):
    barrier = pltpu.get_barrier_semaphore()
    for device in peers:
        pl.semaphore_signal(barrier, inc=1, device_id=device, device_id_type=MESH)
    for condition, device in extra:

        @pl.when(condition)
        def _():
            pl.semaphore_signal(barrier, inc=1, device_id=device, device_id_type=MESH)

    return barrier


class Wire:
    def __init__(self, place, send_sem, recv_sem):
        self.place, self.send_sem, self.recv_sem = place, send_sem, recv_sem
        self.count, self.queue, self.sent, self.free, self.now = 0, [], [], {}, 0.0
        self.count_other = 0

    def send(self, axis, d, src, dst, size, then, late=0.0):
        k = self.count
        self.count += 1
        copy = pltpu.make_async_remote_copy(
            src_ref=src,
            dst_ref=dst,
            send_sem=self.send_sem.at[k],
            recv_sem=self.recv_sem.at[k],
            device_id=self.place.at(axis, d),
            device_id_type=MESH,
        )
        copy.start()
        self.sent.append(copy)
        begin = max(self.now, self.free.get((axis, d), 0.0))
        end = begin + size * 2 / RATE
        self.free[(axis, d)] = end
        heapq.heappush(self.queue, (end + HOP + late, k, copy, then))

    def push(self, when, then):
        self.count_other -= 1
        heapq.heappush(self.queue, (when, self.count_other, None, then))

    def run(self):
        while self.queue:
            when, _, copy, then = heapq.heappop(self.queue)
            self.now = max(self.now, when)
            if copy is not None:
                copy.wait_recv()
            if then is not None:
                then()

    def drain(self):
        for copy in self.sent:
            copy.wait_send()


def gather_kernel(
    tok_t_ref, ids_ref, probs_ref, gate_t_ref, up_t_ref, wd_ref, x_ref, gu_ref, down_ref,
    tok_t, tok_ref, wgu_t, wgu_ref, pieces, own, send_sem, recv_sem, part_send, part_recv, local_sem
):
    p = Place()
    y, z, m = p.y, p.z, p.m
    mine = z == m
    sources = [(y * NZ + m, q) for q in range(NM)]
    targets = [(y * NZ + r, z) for r in range(NZ)]
    neighbours = [p.at(a, d) for a, d in (("x", 1), ("x", -1), ("y", 1), ("y", -1), ("z", 1), ("z", -1), ("c", 1))]
    barrier = greet(
        neighbours, [(jnp.logical_not(jnp.logical_and(mine, m == q)), sources[q]) for q in range(NM)]
    )
    probs = probs_ref[...]
    high = probs.astype(BF).astype(F32)
    middle = (probs - high).astype(BF).astype(F32)
    meta = [ids_ref[...].astype(F32), high, middle, probs - high - middle]
    tok_t[pl.ds(0, LOCAL), :] = tok_t_ref[...]
    tok_t[pl.ds(LOCAL, 64), :] = jnp.concatenate(meta + [jnp.zeros((56, BLOCK), F32)], axis=0).astype(BF)
    tok_ref[...] = tok_t[...].T
    pl.semaphore_wait(barrier, len(neighbours) + NM - mine.astype(jnp.int32))

    for r in range(NZ):
        src = tok_ref.at[pl.ds(r * PIECE, PIECE), :]
        away = jnp.logical_not(jnp.logical_and(mine, z == r))

        @pl.when(away)
        def _():
            pltpu.make_async_remote_copy(
                src_ref=src,
                dst_ref=pieces.at[m],
                send_sem=part_send.at[r],
                recv_sem=part_recv.at[m],
                device_id=targets[r],
                device_id_type=MESH,
            ).start()

        @pl.when(jnp.logical_not(away))
        def _():
            pltpu.make_async_copy(src, pieces.at[m], part_recv.at[m]).start()

    wgu_t[pl.ds(0, 320), pl.ds(0, LOCAL)] = gate_t_ref[...]
    wgu_t[pl.ds(320, 320), pl.ds(0, LOCAL)] = up_t_ref[...]
    wgu_ref[...] = wgu_t[...].T[:LOCAL, :]
    keep_gu = pltpu.make_async_copy(wgu_ref, gu_ref.at[m], local_sem.at[0])
    keep_gu.start()
    keep_down = pltpu.make_async_copy(wd_ref, down_ref.at[m], local_sem.at[1])
    keep_down.start()

    wire = Wire(p, send_sem, recv_sem)

    def weights(own_ref, out, rows, width):
        size = rows * width * 2

        def block(xo, lo, n):
            return out.at[ring(p.x, xo, NX) * 2 + p.c, pl.ds(lo, n), :]

        half = cut_rows(0, rows)

        def share(xo, lo, n):
            at = block(xo, lo, n)
            wire.send("c", 1, at, at, size * n // rows // 4, None, 2 * LATE)

        def arrived(d, xo, lo, n):
            def then():
                if abs(xo) == 1 and (lo, n) == half[0 if d == 1 else 1]:
                    at = block(xo, lo, n)
                    wire.send("x", d, at, at, size * n // rows, arrived(d, xo - d, lo, n), LATE)
                share(xo, lo, n)

            return then

        def begin(first):
            for d in (1, -1):
                lo, n = half[0 if (d == 1) == first else 1]
                src = own_ref.at[pl.ds(lo, n), :]
                wire.send("x", d, src, block(0, lo, n), size * n // rows, arrived(d, -d, lo, n), LATE)
            if first:
                wire.send("c", 1, own_ref, out.at[m], size // 4, None, 2 * LATE)

        return begin

    def cut_rows(lo, n):
        first = (n // 16) // 2 * 16
        return (lo, first), (lo + first, n - first)

    sends = [weights(wgu_ref, gu_ref, LOCAL, 640), weights(wd_ref, down_ref, 320, 512)]

    for q in range(NM):
        pltpu.make_async_copy(pieces.at[q], pieces.at[q], part_recv.at[q]).wait()
    parts = [pieces[q][:, :LOCAL] for q in range(NM)]
    tail = jnp.concatenate([pieces[0][:, LOCAL:], jnp.zeros((PIECE, 64), BF)], axis=1)
    own[...] = jnp.concatenate(parts + [tail], axis=1)

    keep = pltpu.make_async_copy(own, x_ref.at[z, y], local_sem.at[2])
    keep.start()
    wire.now = 6.0
    for first in (True, False):
        for begin in sends:
            begin(first)

    def block(zo, yo, lo, n):
        return x_ref.at[ring(z, zo, NZ), ring(y, yo, NY), :, pl.ds(lo, n)]

    def forward(axis, d, zo, yo, lo, n, src=None):
        dst = block(zo, yo, lo, n)
        wire.send(axis, d, dst if src is None else src, dst, PIECE * n * 2, arrived(axis, d, zo, yo, lo, n))

    def arrived(axis, d, zo, yo, lo, n):
        if axis == "z":
            zo -= d
            dist, far = abs(zo), 4
        else:
            yo -= d
            dist, far = abs(yo), 2

        def then():
            if dist < far - 1:
                forward(axis, d, zo, yo, lo, n)
            elif dist == far - 1:
                low, high = cut(lo, n)
                forward(axis, d, zo, yo, *(low if d == 1 else high))
            if axis == "y" and lo < SPLIT:
                for s in (1, -1):
                    forward("z", s, zo, yo, lo, n)
            if axis == "z" and lo >= SPLIT:
                for s in (1, -1):
                    forward("y", s, zo, yo, lo, n)

        return then

    for axes, lo, n in ((("y", "z"), 0, SPLIT), (("z", "y"), SPLIT, WIDE - SPLIT)):
        for axis in axes:
            for d in (1, -1):
                forward(axis, d, 0, 0, lo, n, own.at[:, pl.ds(lo, n)])
    wire.run()
    keep_gu.wait()
    keep_down.wait()
    keep.wait()
    for r in range(NZ):

        @pl.when(jnp.logical_not(jnp.logical_and(mine, z == r)))
        def _():
            pltpu.make_async_copy(
                tok_ref.at[pl.ds(r * PIECE, PIECE), :], tok_ref.at[pl.ds(r * PIECE, PIECE), :], part_send.at[r]
            ).wait()

    wire.drain()


def spec(space):
    return pl.BlockSpec(memory_space=space)


VM = pltpu.VMEM
ANY = pl.ANY


def params(number, mib):
    return pltpu.CompilerParams(collective_id=number, has_side_effects=True, vmem_limit_bytes=mib * 2**20)


def gather(tok_t, ids, probs, gate_t, up_t, wd):
    return pl.pallas_call(
        gather_kernel,
        name="gather",
        out_shape=(
            jax.ShapeDtypeStruct((NZ, NY, PIECE, WIDE), BF),
            jax.ShapeDtypeStruct((NM, LOCAL, 640), BF),
            jax.ShapeDtypeStruct((NM, 320, LOCAL), BF),
        ),
        in_specs=[spec(VM)] * 6,
        out_specs=[spec(pltpu.HBM)] * 3,
        scratch_shapes=[
            pltpu.VMEM((512, BLOCK), BF),
            pltpu.VMEM((BLOCK, 512), BF),
            pltpu.VMEM((640, 512), BF),
            pltpu.VMEM((LOCAL, 640), BF),
            pltpu.VMEM((NM, PIECE, 512), BF),
            pltpu.VMEM((PIECE, WIDE), BF),
            pltpu.SemaphoreType.DMA((128,)),
            pltpu.SemaphoreType.DMA((128,)),
            pltpu.SemaphoreType.DMA((NZ,)),
            pltpu.SemaphoreType.DMA((NM,)),
            pltpu.SemaphoreType.DMA((3,)),
        ],
        compiler_params=params(0, 59),
    )(tok_t, ids, probs, gate_t, up_t, wd)


ROWS = 2 * SLOTS
OFFSETS = (0, 1, 3, 2)


def experts_kernel(
    place_ref, back_ref, scale_ref, x_hbm, gu_hbm, wd_hbm, eg_hbm, eu_hbm, ed_hbm, out_ref,
    done, s_ref, shared, value, rows, eg, eu, ed, xs, gu, wd, wide, part, from_pair, from_x, held, send_sem, recv_sem, local_sem, load_sem,
):
    p = Place()
    loads = [
        pltpu.make_async_copy(src, dst, load_sem.at[k])
        for k, (src, dst) in enumerate(
            ((x_hbm, xs), (eg_hbm, eg), (eu_hbm, eu), (ed_hbm, ed), (wd_hbm, wd), (gu_hbm, gu))
        )
    ]
    for load in loads:
        load.start()
    neighbours = [p.at("x", 1), p.at("x", -1), p.at("c", 1)]
    barrier = greet(neighbours)
    loads[0].wait()
    s_ref[...] = dot(place_ref[...], xs[:, :FEAT]).astype(BF)
    pl.semaphore_wait(barrier, 3)
    wire = Wire(p, send_sem, recv_sem)
    wire.now = 3.0
    keep = pltpu.make_async_copy(s_ref, rows.at[p.m], local_sem)
    keep.start()
    low, high = cut(0, FEAT)

    def block(xo, lo, n):
        return rows.at[ring(p.x, xo, NX) * 2 + p.c, :, pl.ds(lo, n)]

    def base(xo):
        return ring(p.x, xo, NX) * 2

    missing = {0: 1, 1: 4, 3: 4, 2: 4}

    def landed(xo):
        def then():
            missing[xo] -= 1
            if missing[xo] == 0:
                routed(xo)

        return then

    def share(xo, lo, n):
        wire.send("c", 1, block(xo, lo, n), block(xo, lo, n), SLOTS * n, landed(xo % NX))

    def moved(d, xo, lo, n):
        def then():
            if abs(xo) == 1 and (lo, n) == (low if d == 1 else high):
                dst = block(xo, lo, n)
                wire.send("x", d, dst, dst, SLOTS * n * 2, moved(d, xo - d, lo, n))
                if d == -1:
                    wire.push(wire.now, lambda: filler(1, 1))
            share(xo, lo, n)
            landed(xo % NX)()

        return then

    for first in (True, False):
        for d in (1, -1):
            lo, n = low if (d == 1) == first else high
            wire.send("x", d, s_ref.at[:, pl.ds(lo, n)], block(0, lo, n), SLOTS * n * 2, moved(d, -d, lo, n))
        if first:
            wire.send("c", 1, s_ref, rows.at[p.m], SLOTS * FEAT // 2, landed(0))

    def turned(a, b):
        return lax.dot_general(a, b, (((1,), (1,)), ((), ())), preferred_element_type=F32)

    def routed(xo):
        if xo == 0:
            keep.wait()
            for load in loads[1:4]:
                load.wait()
        chunk = rows[pl.ds(base(xo), 2)].reshape(ROWS, FEAT)
        hidden = (jax.nn.silu(turned(chunk, eg[...])) * turned(chunk, eu[...])).astype(BF)
        part[xo] = dot(hidden, ed[...]).astype(BF).reshape(2, SLOTS, FEAT)
        wire.now += 2.5
        wire.send("c", 1, part.at[xo, 1 - p.c], from_pair.at[xo], SLOTS * FEAT // 2, paired(xo))
        if xo == 0:
            filler(0, 1)
        if xo == 2:
            wire.push(wire.now + 5.0, lambda: filler(2, 2))

    def filler(start, count):
        if start == 0:
            for load in loads[4:]:
                load.wait()
            wide[...] = jnp.concatenate([wd[q] for q in range(NM)], axis=1)

        def body(i, carry):
            at = pl.ds(pl.multiple_of(i * ROWS, ROWS), ROWS)
            both = dot(xs[at, :FEAT], gu[...])
            hidden = (jax.nn.silu(both[:, :320]) * both[:, 320:640]).astype(BF)
            shared[at, :] = dot(hidden, wide[...])
            return carry

        lax.fori_loop(start, start + count, body, 0)
        wire.now += 2.5 * count

    def own_sum(xo):
        return part[xo, p.c].astype(F32) + from_pair[xo].astype(F32)

    ready = {}

    def paired(xo):
        def then():
            if xo == 0:
                return
            held[xo] = own_sum(xo).astype(BF)
            for d in (1, -1):
                lo, n = low if d == 1 else high
                k = 0 if d == 1 else 1
                if xo == 2:
                    at = pl.ds(lo, n)
                    wire.send("x", d, held.at[2, :, at], from_x.at[k, :, at], SLOTS * n * 2, passed(d, lo, n))
                elif xo == d % NX:
                    lo, n = high if d == 1 else low
                    at = pl.ds(lo, n)
                    wire.send("x", d, held.at[xo, :, at], from_x.at[2 + k, :, at], SLOTS * n * 2, None)
                    ready[(d, "pair")] = True
                    onward(d)

        return then

    def passed(d, lo, n):
        def then():
            ready[(d, "far")] = (lo, n)
            onward(d)

        return then

    def onward(d):
        if (d, "pair") not in ready or (d, "far") not in ready:
            return
        slot = d % NX
        lo, n = ready[(d, "far")]
        k = 0 if d == 1 else 1
        at = pl.ds(lo, n)
        total = part[slot, p.c, :, at].astype(F32) + from_pair[slot, :, at].astype(F32) + from_x[k, :, at].astype(F32)
        held[slot, :, at] = total.astype(BF)
        wire.send("x", d, held.at[slot, :, at], from_x.at[2 + k, :, at], SLOTS * n * 2, None)

    wire.run()
    total = own_sum(0) + from_x[2].astype(F32) + from_x[3].astype(F32)
    value[...] = (total * scale_ref[...]).astype(BF)

    def combine(i, carry):
        at = pl.ds(pl.multiple_of(i * ROWS, ROWS), ROWS)
        done[at, :] = (shared[at, :] + dot(back_ref[at, :], value[...])).astype(BF)
        pltpu.make_async_copy(done.at[at, :], out_ref.at[at, :], load_sem.at[i]).start()
        return carry

    lax.fori_loop(0, 4, combine, 0)
    wire.drain()
    for i in range(4):
        at = pl.ds(i * ROWS, ROWS)
        pltpu.make_async_copy(done.at[at, :], out_ref.at[at, :], load_sem.at[i]).wait()


def experts(place, back, scale, x, gu, wd, eg, eu, ed):
    slots = pltpu.VMEM((NX, SLOTS, FEAT), BF)
    return pl.pallas_call(
        experts_kernel,
        name="experts",
        out_shape=jax.ShapeDtypeStruct((4 * BLOCK, FEAT), BF),
        in_specs=[spec(VM)] * 3 + [spec(ANY)] * 6,
        out_specs=spec(ANY),
        scratch_shapes=[
            pltpu.VMEM((4 * BLOCK, FEAT), BF),
            pltpu.VMEM((SLOTS, FEAT), BF),
            pltpu.VMEM((4 * BLOCK, FEAT), F32),
            pltpu.VMEM((SLOTS, FEAT), BF),
            pltpu.VMEM((NM, SLOTS, FEAT), BF),
            pltpu.VMEM((320, FEAT), BF),
            pltpu.VMEM((320, FEAT), BF),
            pltpu.VMEM((320, FEAT), BF),
            pltpu.VMEM((4 * BLOCK, WIDE), BF),
            pltpu.VMEM((FEAT, 640), BF),
            pltpu.VMEM((NM, 320, LOCAL), BF),
            pltpu.VMEM((320, FEAT), BF),
            pltpu.VMEM((NX, 2, SLOTS, FEAT), BF),
            slots,
            slots,
            slots,
            pltpu.SemaphoreType.DMA((32,)),
            pltpu.SemaphoreType.DMA((32,)),
            pltpu.SemaphoreType.DMA,
            pltpu.SemaphoreType.DMA((6,)),
        ],
        compiler_params=params(1, 54),
    )(place, back, scale, x, gu, wd, eg, eu, ed)


def reduce_kernel(
    in_hbm, out_ref, in_ref, held, z_in, y_in, pieces, load_sem, send_sem, recv_sem, part_send, part_recv
):
    p = Place()
    y, z, m = p.y, p.z, p.m
    mine = z == m
    load = pltpu.make_async_copy(in_hbm, in_ref, load_sem)
    load.start()
    sources = [(y * NZ + r, z) for r in range(NZ)]
    targets = [(y * NZ + m, q) for q in range(NM)]
    neighbours = [p.at(a, d) for a, d in (("y", 1), ("y", -1), ("z", 1), ("z", -1))]
    barrier = greet(
        neighbours, [(jnp.logical_not(jnp.logical_and(mine, z == r)), sources[r]) for r in range(NZ)]
    )
    pl.semaphore_wait(barrier, len(neighbours) + NM - mine.astype(jnp.int32))
    load.wait()
    wire = Wire(p, send_sem, recv_sem)

    def index(zo, yo):
        return ring(z, zo, NZ), ring(y, yo, NY)

    sizes = {"z": NZ, "y": NY}
    inbox = {"z": z_in, "y": y_in}

    class Chain:
        def __init__(self, axis, other, lo, n, second, done):
            self.axis, self.other, self.lo, self.n = axis, other, lo, n
            self.second, self.done, self.left = second, done, 2
            self.far = sizes[axis] // 2
            self.ready = {}

        def where(self, o):
            return (o, self.other) if self.axis == "z" else (self.other, o)

        def mailbox(self, d, left, lo, n):
            zo, yo = self.where(0)
            k = (0 if d == 1 else 1) * self.far + left
            other = self.other % (NY if self.axis == "z" else NZ)
            return inbox[self.axis].at[k, other, :, pl.ds(lo, n)]

        def source(self, o, lo, n):
            a, b = index(*self.where(o))
            ref = held if self.second else in_ref
            return ref.at[a, b, :, pl.ds(lo, n)]

        def have(self, o):
            self.ready[o % sizes[self.axis]] = True
            if o % sizes[self.axis] == self.far:
                low, high = cut(self.lo, self.n)
                for d, (lo, n) in ((1, low), (-1, high)):
                    wire.send(
                        self.axis,
                        d,
                        self.source(self.far, lo, n),
                        self.mailbox(d, self.far - 1, lo, n),
                        PIECE * n * 2,
                        self.arrived(d, self.far - 1, lo, n),
                    )
            for d in (1, -1):
                self.step(d, o * d % sizes[self.axis])

        def arrived(self, d, left, lo, n):
            def then():
                self.ready[(d, left)] = (lo, n)
                self.step(d, left)

            return then

        def step(self, d, left):
            size = sizes[self.axis]
            o = d * left
            if left == 0 or left >= self.far:
                if left == 0:
                    self.finish()
                return
            if (d, left) not in self.ready or o % size not in self.ready:
                return
            lo, n = self.ready[(d, left)]
            a, b = index(*self.where(o))
            at = pl.ds(lo, n)
            base = held if self.second else in_ref
            if (lo, n) != (self.lo, self.n) and not self.second:
                rest = [c for c in cut(self.lo, self.n) if c != (lo, n)][0]
                held[a, b, :, pl.ds(*rest)] = in_ref[a, b, :, pl.ds(*rest)]
            total = base[a, b, :, at].astype(F32) + self.mailbox(d, left, lo, n)[...].astype(F32)
            held[a, b, :, at] = total.astype(BF)
            wire.send(
                self.axis,
                d,
                held.at[a, b, :, pl.ds(self.lo, self.n)],
                self.mailbox(d, left - 1, self.lo, self.n),
                PIECE * self.n * 2,
                self.arrived(d, left - 1, self.lo, self.n),
            )

        def finish(self):
            if (1, 0) not in self.ready or (-1, 0) not in self.ready or 0 not in self.ready or self.left == 0:
                return
            self.left = 0
            a, b = index(*self.where(0))
            at = pl.ds(self.lo, self.n)
            base = held if self.second else in_ref
            total = base[a, b, :, at].astype(F32)
            for d in (1, -1):
                total = total + self.mailbox(d, 0, self.lo, self.n)[...].astype(F32)
            if not self.second:
                held[a, b, :, at] = total.astype(BF)
            self.done(total)

    last = {}

    def plan(first, second, lo, n):
        def store(total):
            last[lo] = total

        final = Chain(second, 0, lo, n, True, store)
        far = sizes[second] // 2
        offsets = sorted(range(sizes[second]), key=lambda o: (-min(o, sizes[second] - o), o))
        chains = []
        for o in offsets:
            signed = o if o <= far else o - sizes[second]
            chains.append(Chain(first, signed, lo, n, False, lambda total, s=signed: final.have(s)))
        return chains

    groups = [plan("z", "y", 0, SPLIT), plan("y", "z", SPLIT, FEAT - SPLIT)]
    for group in groups:
        for chain in group:
            far = chain.far
            order = [far] + [s * d for d in range(far - 1, 0, -1) for s in (1, -1)] + [0]
            for o in order:
                chain.have(o)
    wire.run()
    whole = jnp.concatenate([last[0], last[SPLIT]], axis=1).astype(BF)
    for q in range(NM):
        pieces[q] = whole[:, q * LOCAL : (q + 1) * LOCAL]
    rows = pl.ds(pl.multiple_of(z * PIECE, PIECE), PIECE)
    for q in range(NM):
        away = jnp.logical_not(jnp.logical_and(mine, m == q))

        @pl.when(away)
        def _():
            pltpu.make_async_remote_copy(
                src_ref=pieces.at[q],
                dst_ref=out_ref.at[rows, :],
                send_sem=part_send.at[q],
                recv_sem=part_recv.at[z],
                device_id=targets[q],
                device_id_type=MESH,
            ).start()

        @pl.when(jnp.logical_not(away))
        def _():
            pltpu.make_async_copy(pieces.at[q], out_ref.at[rows, :], part_recv.at[z]).start()

    for r in range(NZ):
        pltpu.make_async_copy(pieces.at[r], pieces.at[r], part_recv.at[r]).wait()
    for q in range(NM):

        @pl.when(jnp.logical_not(jnp.logical_and(mine, m == q)))
        def _():
            pltpu.make_async_copy(pieces.at[q], pieces.at[q], part_send.at[q]).wait()

    wire.drain()


def reduce_out(partial):
    return pl.pallas_call(
        reduce_kernel,
        name="reduce_out",
        out_shape=jax.ShapeDtypeStruct((BLOCK, LOCAL), BF),
        in_specs=[spec(ANY)],
        out_specs=spec(VM),
        scratch_shapes=[
            pltpu.VMEM((NZ, NY, PIECE, FEAT), BF),
            pltpu.VMEM((NZ, NY, PIECE, FEAT), BF),
            pltpu.VMEM((2 * (NZ // 2), NY, PIECE, FEAT), BF),
            pltpu.VMEM((2 * (NY // 2), NZ, PIECE, FEAT), BF),
            pltpu.VMEM((NM, PIECE, LOCAL), BF),
            pltpu.SemaphoreType.DMA,
            pltpu.SemaphoreType.DMA((96,)),
            pltpu.SemaphoreType.DMA((96,)),
            pltpu.SemaphoreType.DMA((NM,)),
            pltpu.SemaphoreType.DMA((NZ,)),
        ],
        compiler_params=params(2, 59),
    )(partial)


def dot(a, b):
    return jnp.dot(a, b, preferred_element_type=F32)


def on_device(tokens, assignments, gate_probs, expert_gate, expert_up, expert_down, shared_gate, shared_up, shared_down):
    me = lax.axis_index("expert").astype(F32)
    x, gu, down = gather(tokens.T, assignments.T, gate_probs.T, shared_gate.T, shared_up.T, shared_down)
    wide_x = x.reshape(NZ * NY * PIECE, WIDE)
    info = wide_x[:, FEAT : FEAT + 8].astype(F32)
    rows = wide_x.shape[0]

    named = (info[:, 0:2] == me).astype(F32)
    hit = named[:, 0] + named[:, 1]
    weight = named[:, 0] * (info[:, 2] + info[:, 4] + info[:, 6]) + named[:, 1] * (info[:, 3] + info[:, 5] + info[:, 7])
    t = jnp.arange(rows, dtype=jnp.int32)
    group = (t // PIECE) % NY
    before = ((t[:, None] < t[None, :]) & (group[:, None] == group[None, :])).astype(BF)
    rank = dot(hit.astype(BF)[None, :], before)[0]
    slot = jnp.where(hit > 0, group * 16 + rank.astype(jnp.int32), -1)
    place = slot[None, :] == jnp.arange(SLOTS, dtype=jnp.int32)[:, None]

    scale = jnp.sum(place.astype(F32) * weight[None, :], axis=1)
    back = slot[:, None] == jnp.arange(SLOTS, dtype=jnp.int32)[None, :]
    partial = experts(
        place.astype(BF),
        back.astype(BF),
        scale[:, None],
        wide_x,
        gu.reshape(FEAT, 640),
        down,
        jnp.swapaxes(expert_gate[0], 0, 1),
        jnp.swapaxes(expert_up[0], 0, 1),
        expert_down[0],
    )
    return reduce_out(partial.reshape(NZ, NY, PIECE, FEAT))


def solution(mesh):
    placed = (
        P("expert", "mp"),
        P("expert", None),
        P("expert", None),
        P("expert", None, "mp"),
        P("expert", None, "mp"),
        P("expert", "mp", None),
        P("mp", "expert"),
        P("mp", "expert"),
        P("expert", "mp"),
    )
    return jax.shard_map(on_device, mesh=mesh, in_specs=placed, out_specs=P("expert", "mp"), check_vma=False)
```

```python
import heapq

import jax
import jax.numpy as jnp
from jax import lax
from jax.experimental import pallas as pl
from jax.experimental.pallas import tpu as pltpu
from jax.sharding import PartitionSpec as P

MESH = pl.DeviceIdType.MESH
BF = jnp.bfloat16
F32 = jnp.float32
NY, NZ, NX, NM = 4, 8, 4, 8
BLOCK = 128
PIECE = 16
FEAT = 3584
LOCAL = 448
WIDE = FEAT + 128
SLOTS = 64
SPLIT = 1536
RATE = 92e3
HOP = 2.6
LATE = 4.0


def cut(lo, n):
    first = (n // 128) // 2 * 128
    return (lo, first), (lo + first, n - first)


def ring(index, offset, size):
    return lax.rem(index + (offset + size) % size, size)


class Place:
    def __init__(self):
        e = lax.axis_index("expert")
        self.m = lax.axis_index("mp")
        self.y, self.z = lax.div(e, NZ), lax.rem(e, NZ)
        self.x, self.c = lax.div(self.m, 2), lax.rem(self.m, 2)

    def at(self, axis, d):
        y, z, m = self.y, self.z, self.m
        if axis == "y":
            y = ring(y, d, NY)
        elif axis == "z":
            z = ring(z, d, NZ)
        elif axis == "x":
            m = ring(self.x, d, NX) * 2 + self.c
        else:
            m = self.x * 2 + 1 - self.c
        return (y * NZ + z, m)


def greet(peers, extra=()):
    barrier = pltpu.get_barrier_semaphore()
    for device in peers:
        pl.semaphore_signal(barrier, inc=1, device_id=device, device_id_type=MESH)
    for condition, device in extra:

        @pl.when(condition)
        def _():
            pl.semaphore_signal(barrier, inc=1, device_id=device, device_id_type=MESH)

    return barrier


class Wire:
    def __init__(self, place, send_sem, recv_sem):
        self.place, self.send_sem, self.recv_sem = place, send_sem, recv_sem
        self.count, self.queue, self.sent, self.free, self.now = 0, [], [], {}, 0.0
        self.count_other = 0

    def send(self, axis, d, src, dst, size, then, late=0.0):
        k = self.count
        self.count += 1
        copy = pltpu.make_async_remote_copy(
            src_ref=src,
            dst_ref=dst,
            send_sem=self.send_sem.at[k],
            recv_sem=self.recv_sem.at[k],
            device_id=self.place.at(axis, d),
            device_id_type=MESH,
        )
        copy.start()
        self.sent.append(copy)
        begin = max(self.now, self.free.get((axis, d), 0.0))
        end = begin + size * 2 / RATE
        self.free[(axis, d)] = end
        heapq.heappush(self.queue, (end + HOP + late, k, copy, then))

    def push(self, when, then):
        self.count_other -= 1
        heapq.heappush(self.queue, (when, self.count_other, None, then))

    def run(self):
        while self.queue:
            when, _, copy, then = heapq.heappop(self.queue)
            self.now = max(self.now, when)
            if copy is not None:
                copy.wait_recv()
            if then is not None:
                then()

    def drain(self):
        for copy in self.sent:
            copy.wait_send()


def gather_kernel(
    tok_t_ref, ids_ref, probs_ref, gate_t_ref, up_t_ref, wd_ref, x_ref, gu_ref, down_ref,
    tok_t, tok_ref, wgu_t, wgu_ref, pieces, own, send_sem, recv_sem, part_send, part_recv, local_sem
):
    p = Place()
    y, z, m = p.y, p.z, p.m
    mine = z == m
    sources = [(y * NZ + m, q) for q in range(NM)]
    targets = [(y * NZ + r, z) for r in range(NZ)]
    neighbours = [p.at(a, d) for a, d in (("x", 1), ("x", -1), ("y", 1), ("y", -1), ("z", 1), ("z", -1), ("c", 1))]
    barrier = greet(
        neighbours, [(jnp.logical_not(jnp.logical_and(mine, m == q)), sources[q]) for q in range(NM)]
    )
    probs = probs_ref[...]
    high = probs.astype(BF).astype(F32)
    middle = (probs - high).astype(BF).astype(F32)
    meta = [ids_ref[...].astype(F32), high, middle, probs - high - middle]
    tok_t[pl.ds(0, LOCAL), :] = tok_t_ref[...]
    tok_t[pl.ds(LOCAL, 64), :] = jnp.concatenate(meta + [jnp.zeros((56, BLOCK), F32)], axis=0).astype(BF)
    tok_ref[...] = tok_t[...].T
    pl.semaphore_wait(barrier, len(neighbours) + NM - mine.astype(jnp.int32))

    for r in range(NZ):
        src = tok_ref.at[pl.ds(r * PIECE, PIECE), :]
        away = jnp.logical_not(jnp.logical_and(mine, z == r))

        @pl.when(away)
        def _():
            pltpu.make_async_remote_copy(
                src_ref=src,
                dst_ref=pieces.at[m],
                send_sem=part_send.at[r],
                recv_sem=part_recv.at[m],
                device_id=targets[r],
                device_id_type=MESH,
            ).start()

        @pl.when(jnp.logical_not(away))
        def _():
            pltpu.make_async_copy(src, pieces.at[m], part_recv.at[m]).start()

    wgu_t[pl.ds(0, 320), pl.ds(0, LOCAL)] = gate_t_ref[...]
    wgu_t[pl.ds(320, 320), pl.ds(0, LOCAL)] = up_t_ref[...]
    wgu_ref[...] = wgu_t[...].T[:LOCAL, :]
    keep_gu = pltpu.make_async_copy(wgu_ref, gu_ref.at[m], local_sem.at[0])
    keep_gu.start()
    keep_down = pltpu.make_async_copy(wd_ref, down_ref.at[m], local_sem.at[1])
    keep_down.start()

    wire = Wire(p, send_sem, recv_sem)

    def weights(own_ref, out, rows, width):
        size = rows * width * 2

        def block(xo, lo, n):
            return out.at[ring(p.x, xo, NX) * 2 + p.c, pl.ds(lo, n), :]

        half = cut_rows(0, rows)

        def share(xo, lo, n):
            at = block(xo, lo, n)
            wire.send("c", 1, at, at, size * n // rows // 4, None, 2 * LATE)

        def arrived(d, xo, lo, n):
            def then():
                if abs(xo) == 1 and (lo, n) == half[0 if d == 1 else 1]:
                    at = block(xo, lo, n)
                    wire.send("x", d, at, at, size * n // rows, arrived(d, xo - d, lo, n), LATE)
                share(xo, lo, n)

            return then

        def begin(first):
            for d in (1, -1):
                lo, n = half[0 if (d == 1) == first else 1]
                src = own_ref.at[pl.ds(lo, n), :]
                wire.send("x", d, src, block(0, lo, n), size * n // rows, arrived(d, -d, lo, n), LATE)
            if first:
                wire.send("c", 1, own_ref, out.at[m], size // 4, None, 2 * LATE)

        return begin

    def cut_rows(lo, n):
        first = (n // 16) // 2 * 16
        return (lo, first), (lo + first, n - first)

    sends = [weights(wgu_ref, gu_ref, LOCAL, 640), weights(wd_ref, down_ref, 320, 512)]

    for q in range(NM):
        pltpu.make_async_copy(pieces.at[q], pieces.at[q], part_recv.at[q]).wait()
    parts = [pieces[q][:, :LOCAL] for q in range(NM)]
    tail = jnp.concatenate([pieces[0][:, LOCAL:], jnp.zeros((PIECE, 64), BF)], axis=1)
    own[...] = jnp.concatenate(parts + [tail], axis=1)

    keep = pltpu.make_async_copy(own, x_ref.at[z, y], local_sem.at[2])
    keep.start()
    wire.now = 6.0
    for first in (True, False):
        for begin in sends:
            begin(first)

    def block(zo, yo, lo, n):
        return x_ref.at[ring(z, zo, NZ), ring(y, yo, NY), :, pl.ds(lo, n)]

    def forward(axis, d, zo, yo, lo, n, src=None):
        dst = block(zo, yo, lo, n)
        wire.send(axis, d, dst if src is None else src, dst, PIECE * n * 2, arrived(axis, d, zo, yo, lo, n))

    def arrived(axis, d, zo, yo, lo, n):
        if axis == "z":
            zo -= d
            dist, far = abs(zo), 4
        else:
            yo -= d
            dist, far = abs(yo), 2

        def then():
            if dist < far - 1:
                forward(axis, d, zo, yo, lo, n)
            elif dist == far - 1:
                low, high = cut(lo, n)
                forward(axis, d, zo, yo, *(low if d == 1 else high))
            if axis == "y" and lo < SPLIT:
                for s in (1, -1):
                    forward("z", s, zo, yo, lo, n)
            if axis == "z" and lo >= SPLIT:
                for s in (1, -1):
                    forward("y", s, zo, yo, lo, n)

        return then

    for axes, lo, n in ((("y", "z"), 0, SPLIT), (("z", "y"), SPLIT, WIDE - SPLIT)):
        for axis in axes:
            for d in (1, -1):
                forward(axis, d, 0, 0, lo, n, own.at[:, pl.ds(lo, n)])
    wire.run()
    keep_gu.wait()
    keep_down.wait()
    keep.wait()
    for r in range(NZ):

        @pl.when(jnp.logical_not(jnp.logical_and(mine, z == r)))
        def _():
            pltpu.make_async_copy(
                tok_ref.at[pl.ds(r * PIECE, PIECE), :], tok_ref.at[pl.ds(r * PIECE, PIECE), :], part_send.at[r]
            ).wait()

    wire.drain()


def spec(space):
    return pl.BlockSpec(memory_space=space)


VM = pltpu.VMEM
ANY = pl.ANY


def params(number, mib):
    return pltpu.CompilerParams(collective_id=number, has_side_effects=True, vmem_limit_bytes=mib * 2**20)


def gather(tok_t, ids, probs, gate_t, up_t, wd):
    return pl.pallas_call(
        gather_kernel,
        name="gather",
        out_shape=(
            jax.ShapeDtypeStruct((NZ, NY, PIECE, WIDE), BF),
            jax.ShapeDtypeStruct((NM, LOCAL, 640), BF),
            jax.ShapeDtypeStruct((NM, 320, LOCAL), BF),
        ),
        in_specs=[spec(VM)] * 6,
        out_specs=[spec(pltpu.HBM)] * 3,
        scratch_shapes=[
            pltpu.VMEM((512, BLOCK), BF),
            pltpu.VMEM((BLOCK, 512), BF),
            pltpu.VMEM((640, 512), BF),
            pltpu.VMEM((LOCAL, 640), BF),
            pltpu.VMEM((NM, PIECE, 512), BF),
            pltpu.VMEM((PIECE, WIDE), BF),
            pltpu.SemaphoreType.DMA((128,)),
            pltpu.SemaphoreType.DMA((128,)),
            pltpu.SemaphoreType.DMA((NZ,)),
            pltpu.SemaphoreType.DMA((NM,)),
            pltpu.SemaphoreType.DMA((3,)),
        ],
        compiler_params=params(0, 59),
    )(tok_t, ids, probs, gate_t, up_t, wd)


ROWS = 2 * SLOTS
OFFSETS = (0, 1, 3, 2)


def experts_kernel(
    x_hbm, gu_hbm, wd_hbm, eg_hbm, eu_hbm, ed_hbm, out_ref,
    back_ref, scale_ref, done, s_ref, shared, value, rows, eg, eu, ed, xs, gu, wd, wide, part, from_pair, from_x, held, send_sem, recv_sem, local_sem, load_sem,
):
    p = Place()
    loads = [
        pltpu.make_async_copy(src, dst, load_sem.at[k])
        for k, (src, dst) in enumerate(
            ((x_hbm, xs), (eg_hbm, eg), (eu_hbm, eu), (ed_hbm, ed), (wd_hbm, wd), (gu_hbm, gu))
        )
    ]
    for load in loads:
        load.start()
    neighbours = [p.at("x", 1), p.at("x", -1), p.at("c", 1)]
    barrier = greet(neighbours)
    loads[0].wait()
    tokens = 4 * BLOCK
    info = xs[:, FEAT:].astype(F32)
    me = lax.axis_index("expert").astype(F32)

    def column(k):
        return info[:, k : k + 1]

    named = [jnp.where(column(k) == me, 1.0, 0.0) for k in range(2)]
    hit = named[0] + named[1]
    weight = sum(named[k] * (column(2 + k) + column(4 + k) + column(6 + k)) for k in range(2))
    t = lax.broadcasted_iota(jnp.int32, (tokens, tokens), 0)
    u = lax.broadcasted_iota(jnp.int32, (tokens, tokens), 1)
    same = lax.rem(lax.div(t, PIECE), NY) == lax.rem(lax.div(u, PIECE), NY)
    before = jnp.where(jnp.logical_and(same, u < t), 1.0, 0.0).astype(BF)
    rank = dot(before, jnp.broadcast_to(hit, (tokens, 128)).astype(BF))
    row = lax.broadcasted_iota(jnp.int32, (tokens, 128), 0)
    lane = lax.broadcasted_iota(jnp.int32, (tokens, 128), 1)
    slot = rank + (lax.rem(lax.div(row, PIECE), NY) * 16).astype(F32)
    back = jnp.where(slot == lane.astype(F32), jnp.broadcast_to(hit, (tokens, 128)), 0.0)
    back_ref[...] = back.astype(BF)
    scale_ref[...] = jnp.sum((back * weight).T, axis=1, keepdims=True)[:SLOTS]
    s_ref[...] = dot(back.T[:SLOTS].astype(BF), xs[:, :FEAT]).astype(BF)
    pl.semaphore_wait(barrier, 3)
    wire = Wire(p, send_sem, recv_sem)
    wire.now = 3.0
    keep = pltpu.make_async_copy(s_ref, rows.at[p.m], local_sem)
    keep.start()
    low, high = cut(0, FEAT)

    def block(xo, lo, n):
        return rows.at[ring(p.x, xo, NX) * 2 + p.c, :, pl.ds(lo, n)]

    def base(xo):
        return ring(p.x, xo, NX) * 2

    missing = {0: 1, 1: 4, 3: 4, 2: 4}

    def landed(xo):
        def then():
            missing[xo] -= 1
            if missing[xo] == 0:
                routed(xo)

        return then

    def share(xo, lo, n):
        wire.send("c", 1, block(xo, lo, n), block(xo, lo, n), SLOTS * n, landed(xo % NX))

    def moved(d, xo, lo, n):
        def then():
            if abs(xo) == 1 and (lo, n) == (low if d == 1 else high):
                dst = block(xo, lo, n)
                wire.send("x", d, dst, dst, SLOTS * n * 2, moved(d, xo - d, lo, n))
                if d == -1:
                    wire.push(wire.now, lambda: filler(1, 1))
            share(xo, lo, n)
            landed(xo % NX)()

        return then

    for first in (True, False):
        for d in (1, -1):
            lo, n = low if (d == 1) == first else high
            wire.send("x", d, s_ref.at[:, pl.ds(lo, n)], block(0, lo, n), SLOTS * n * 2, moved(d, -d, lo, n))
        if first:
            wire.send("c", 1, s_ref, rows.at[p.m], SLOTS * FEAT // 2, landed(0))

    def turned(a, b):
        return lax.dot_general(a, b, (((1,), (1,)), ((), ())), preferred_element_type=F32)

    def routed(xo):
        if xo == 0:
            keep.wait()
            for load in loads[1:4]:
                load.wait()
        chunk = rows[pl.ds(base(xo), 2)].reshape(ROWS, FEAT)
        hidden = (jax.nn.silu(turned(chunk, eg[...])) * turned(chunk, eu[...])).astype(BF)
        part[xo] = dot(hidden, ed[...]).astype(BF).reshape(2, SLOTS, FEAT)
        wire.now += 2.5
        wire.send("c", 1, part.at[xo, 1 - p.c], from_pair.at[xo], SLOTS * FEAT // 2, paired(xo))
        if xo == 0:
            filler(0, 1)
        if xo == 2:
            wire.push(wire.now + 5.0, lambda: filler(2, 2))

    def filler(start, count):
        if start == 0:
            for load in loads[4:]:
                load.wait()
            wide[...] = jnp.concatenate([wd[q] for q in range(NM)], axis=1)

        def body(i, carry):
            at = pl.ds(pl.multiple_of(i * ROWS, ROWS), ROWS)
            both = dot(xs[at, :FEAT], gu[...])
            hidden = (jax.nn.silu(both[:, :320]) * both[:, 320:640]).astype(BF)
            shared[at, :] = dot(hidden, wide[...])
            return carry

        lax.fori_loop(start, start + count, body, 0)
        wire.now += 2.5 * count

    def own_sum(xo):
        return part[xo, p.c].astype(F32) + from_pair[xo].astype(F32)

    ready = {}

    def paired(xo):
        def then():
            if xo == 0:
                return
            held[xo] = own_sum(xo).astype(BF)
            for d in (1, -1):
                lo, n = low if d == 1 else high
                k = 0 if d == 1 else 1
                if xo == 2:
                    at = pl.ds(lo, n)
                    wire.send("x", d, held.at[2, :, at], from_x.at[k, :, at], SLOTS * n * 2, passed(d, lo, n))
                elif xo == d % NX:
                    lo, n = high if d == 1 else low
                    at = pl.ds(lo, n)
                    wire.send("x", d, held.at[xo, :, at], from_x.at[2 + k, :, at], SLOTS * n * 2, None)
                    ready[(d, "pair")] = True
                    onward(d)

        return then

    def passed(d, lo, n):
        def then():
            ready[(d, "far")] = (lo, n)
            onward(d)

        return then

    def onward(d):
        if (d, "pair") not in ready or (d, "far") not in ready:
            return
        slot = d % NX
        lo, n = ready[(d, "far")]
        k = 0 if d == 1 else 1
        at = pl.ds(lo, n)
        total = part[slot, p.c, :, at].astype(F32) + from_pair[slot, :, at].astype(F32) + from_x[k, :, at].astype(F32)
        held[slot, :, at] = total.astype(BF)
        wire.send("x", d, held.at[slot, :, at], from_x.at[2 + k, :, at], SLOTS * n * 2, None)

    wire.run()
    total = own_sum(0) + from_x[2].astype(F32) + from_x[3].astype(F32)
    value[...] = (total * scale_ref[...]).astype(BF)

    def combine(i, carry):
        at = pl.ds(pl.multiple_of(i * ROWS, ROWS), ROWS)
        done[at, :] = (shared[at, :] + dot(back_ref[at, :SLOTS], value[...])).astype(BF)
        pltpu.make_async_copy(done.at[at, :], out_ref.at[at, :], load_sem.at[i]).start()
        return carry

    lax.fori_loop(0, 4, combine, 0)
    wire.drain()
    for i in range(4):
        at = pl.ds(i * ROWS, ROWS)
        pltpu.make_async_copy(done.at[at, :], out_ref.at[at, :], load_sem.at[i]).wait()


def experts(x, gu, wd, eg, eu, ed):
    slots = pltpu.VMEM((NX, SLOTS, FEAT), BF)
    return pl.pallas_call(
        experts_kernel,
        name="experts",
        out_shape=jax.ShapeDtypeStruct((4 * BLOCK, FEAT), BF),
        in_specs=[spec(ANY)] * 6,
        out_specs=spec(ANY),
        scratch_shapes=[
            pltpu.VMEM((4 * BLOCK, 128), BF),
            pltpu.VMEM((SLOTS, 1), F32),
            pltpu.VMEM((4 * BLOCK, FEAT), BF),
            pltpu.VMEM((SLOTS, FEAT), BF),
            pltpu.VMEM((4 * BLOCK, FEAT), F32),
            pltpu.VMEM((SLOTS, FEAT), BF),
            pltpu.VMEM((NM, SLOTS, FEAT), BF),
            pltpu.VMEM((320, FEAT), BF),
            pltpu.VMEM((320, FEAT), BF),
            pltpu.VMEM((320, FEAT), BF),
            pltpu.VMEM((4 * BLOCK, WIDE), BF),
            pltpu.VMEM((FEAT, 640), BF),
            pltpu.VMEM((NM, 320, LOCAL), BF),
            pltpu.VMEM((320, FEAT), BF),
            pltpu.VMEM((NX, 2, SLOTS, FEAT), BF),
            slots,
            slots,
            slots,
            pltpu.SemaphoreType.DMA((32,)),
            pltpu.SemaphoreType.DMA((32,)),
            pltpu.SemaphoreType.DMA,
            pltpu.SemaphoreType.DMA((6,)),
        ],
        compiler_params=params(1, 54),
    )(x, gu, wd, eg, eu, ed)


def reduce_kernel(
    in_hbm, out_ref, in_ref, held, z_in, y_in, pieces, load_sem, send_sem, recv_sem, part_send, part_recv
):
    p = Place()
    y, z, m = p.y, p.z, p.m
    mine = z == m
    load = pltpu.make_async_copy(in_hbm, in_ref, load_sem)
    load.start()
    sources = [(y * NZ + r, z) for r in range(NZ)]
    targets = [(y * NZ + m, q) for q in range(NM)]
    neighbours = [p.at(a, d) for a, d in (("y", 1), ("y", -1), ("z", 1), ("z", -1))]
    barrier = greet(
        neighbours, [(jnp.logical_not(jnp.logical_and(mine, z == r)), sources[r]) for r in range(NZ)]
    )
    pl.semaphore_wait(barrier, len(neighbours) + NM - mine.astype(jnp.int32))
    load.wait()
    wire = Wire(p, send_sem, recv_sem)

    def index(zo, yo):
        return ring(z, zo, NZ), ring(y, yo, NY)

    sizes = {"z": NZ, "y": NY}
    inbox = {"z": z_in, "y": y_in}

    class Chain:
        def __init__(self, axis, other, lo, n, second, done):
            self.axis, self.other, self.lo, self.n = axis, other, lo, n
            self.second, self.done, self.left = second, done, 2
            self.far = sizes[axis] // 2
            self.ready = {}

        def where(self, o):
            return (o, self.other) if self.axis == "z" else (self.other, o)

        def mailbox(self, d, left, lo, n):
            zo, yo = self.where(0)
            k = (0 if d == 1 else 1) * self.far + left
            other = self.other % (NY if self.axis == "z" else NZ)
            return inbox[self.axis].at[k, other, :, pl.ds(lo, n)]

        def source(self, o, lo, n):
            a, b = index(*self.where(o))
            ref = held if self.second else in_ref
            return ref.at[a, b, :, pl.ds(lo, n)]

        def have(self, o):
            self.ready[o % sizes[self.axis]] = True
            if o % sizes[self.axis] == self.far:
                low, high = cut(self.lo, self.n)
                for d, (lo, n) in ((1, low), (-1, high)):
                    wire.send(
                        self.axis,
                        d,
                        self.source(self.far, lo, n),
                        self.mailbox(d, self.far - 1, lo, n),
                        PIECE * n * 2,
                        self.arrived(d, self.far - 1, lo, n),
                    )
            for d in (1, -1):
                self.step(d, o * d % sizes[self.axis])

        def arrived(self, d, left, lo, n):
            def then():
                self.ready[(d, left)] = (lo, n)
                self.step(d, left)

            return then

        def step(self, d, left):
            size = sizes[self.axis]
            o = d * left
            if left == 0 or left >= self.far:
                if left == 0:
                    self.finish()
                return
            if (d, left) not in self.ready or o % size not in self.ready:
                return
            lo, n = self.ready[(d, left)]
            a, b = index(*self.where(o))
            at = pl.ds(lo, n)
            base = held if self.second else in_ref
            if (lo, n) != (self.lo, self.n) and not self.second:
                rest = [c for c in cut(self.lo, self.n) if c != (lo, n)][0]
                held[a, b, :, pl.ds(*rest)] = in_ref[a, b, :, pl.ds(*rest)]
            total = base[a, b, :, at].astype(F32) + self.mailbox(d, left, lo, n)[...].astype(F32)
            held[a, b, :, at] = total.astype(BF)
            wire.send(
                self.axis,
                d,
                held.at[a, b, :, pl.ds(self.lo, self.n)],
                self.mailbox(d, left - 1, self.lo, self.n),
                PIECE * self.n * 2,
                self.arrived(d, left - 1, self.lo, self.n),
            )

        def finish(self):
            if (1, 0) not in self.ready or (-1, 0) not in self.ready or 0 not in self.ready or self.left == 0:
                return
            self.left = 0
            a, b = index(*self.where(0))
            at = pl.ds(self.lo, self.n)
            base = held if self.second else in_ref
            total = base[a, b, :, at].astype(F32)
            for d in (1, -1):
                total = total + self.mailbox(d, 0, self.lo, self.n)[...].astype(F32)
            if not self.second:
                held[a, b, :, at] = total.astype(BF)
            self.done(total)

    last = {}

    def plan(first, second, lo, n):
        def store(total):
            last[lo] = total

        final = Chain(second, 0, lo, n, True, store)
        far = sizes[second] // 2
        offsets = sorted(range(sizes[second]), key=lambda o: (-min(o, sizes[second] - o), o))
        chains = []
        for o in offsets:
            signed = o if o <= far else o - sizes[second]
            chains.append(Chain(first, signed, lo, n, False, lambda total, s=signed: final.have(s)))
        return chains

    groups = [plan("z", "y", 0, SPLIT), plan("y", "z", SPLIT, FEAT - SPLIT)]
    for group in groups:
        for chain in group:
            far = chain.far
            order = [far] + [s * d for d in range(far - 1, 0, -1) for s in (1, -1)] + [0]
            for o in order:
                chain.have(o)
    wire.run()
    whole = jnp.concatenate([last[0], last[SPLIT]], axis=1).astype(BF)
    for q in range(NM):
        pieces[q] = whole[:, q * LOCAL : (q + 1) * LOCAL]
    rows = pl.ds(pl.multiple_of(z * PIECE, PIECE), PIECE)
    for q in range(NM):
        away = jnp.logical_not(jnp.logical_and(mine, m == q))

        @pl.when(away)
        def _():
            pltpu.make_async_remote_copy(
                src_ref=pieces.at[q],
                dst_ref=out_ref.at[rows, :],
                send_sem=part_send.at[q],
                recv_sem=part_recv.at[z],
                device_id=targets[q],
                device_id_type=MESH,
            ).start()

        @pl.when(jnp.logical_not(away))
        def _():
            pltpu.make_async_copy(pieces.at[q], out_ref.at[rows, :], part_recv.at[z]).start()

    for r in range(NZ):
        pltpu.make_async_copy(pieces.at[r], pieces.at[r], part_recv.at[r]).wait()
    for q in range(NM):

        @pl.when(jnp.logical_not(jnp.logical_and(mine, m == q)))
        def _():
            pltpu.make_async_copy(pieces.at[q], pieces.at[q], part_send.at[q]).wait()

    wire.drain()


def reduce_out(partial):
    return pl.pallas_call(
        reduce_kernel,
        name="reduce_out",
        out_shape=jax.ShapeDtypeStruct((BLOCK, LOCAL), BF),
        in_specs=[spec(ANY)],
        out_specs=spec(VM),
        scratch_shapes=[
            pltpu.VMEM((NZ, NY, PIECE, FEAT), BF),
            pltpu.VMEM((NZ, NY, PIECE, FEAT), BF),
            pltpu.VMEM((2 * (NZ // 2), NY, PIECE, FEAT), BF),
            pltpu.VMEM((2 * (NY // 2), NZ, PIECE, FEAT), BF),
            pltpu.VMEM((NM, PIECE, LOCAL), BF),
            pltpu.SemaphoreType.DMA,
            pltpu.SemaphoreType.DMA((96,)),
            pltpu.SemaphoreType.DMA((96,)),
            pltpu.SemaphoreType.DMA((NM,)),
            pltpu.SemaphoreType.DMA((NZ,)),
        ],
        compiler_params=params(2, 57),
    )(partial)


def dot(a, b):
    return jnp.dot(a, b, preferred_element_type=F32)


def on_device(tokens, assignments, gate_probs, expert_gate, expert_up, expert_down, shared_gate, shared_up, shared_down):
    x, gu, down = gather(tokens.T, assignments.T, gate_probs.T, shared_gate.T, shared_up.T, shared_down)
    partial = experts(
        x.reshape(NZ * NY * PIECE, WIDE),
        gu.reshape(FEAT, 640),
        down,
        jnp.swapaxes(expert_gate[0], 0, 1),
        jnp.swapaxes(expert_up[0], 0, 1),
        expert_down[0],
    )
    return reduce_out(partial.reshape(NZ, NY, PIECE, FEAT))


def solution(mesh):
    placed = (
        P("expert", "mp"),
        P("expert", None),
        P("expert", None),
        P("expert", None, "mp"),
        P("expert", None, "mp"),
        P("expert", "mp", None),
        P("mp", "expert"),
        P("mp", "expert"),
        P("expert", "mp"),
    )
    return jax.shard_map(on_device, mesh=mesh, in_specs=placed, out_specs=P("expert", "mp"), check_vma=False)
```
